128 devices in a mesh: shot: 16 (over z, x_hi, core), tile: 8 (over x_lo, y).
Axes of the slice: x: 4 (x_hi: 2, x_lo: 2; x = x_hi * 2 + x_lo), y: 4, z: 4, core: 2. Of those that a mesh axis runs over, the one named last changes fastest.
Arguments:
- lame_lambda: float32 [512, 32, 256], P(('shot', 'tile')), may hold values from 1 to 2
- lame_mu: float32 [512, 32, 256], P(('shot', 'tile')), may hold values from 0.5 to 1
- buoyancy: float32 [512, 32, 256], P(('shot', 'tile')), may hold values from 0.5 to 1
- aperture_row: int32 [16], replicated, may hold values from 0 to 15
- wave_state: float32 [16, 9, 32, 32, 256], P('shot', None, 'tile'), may hold values from -6 to 6
- source_cell: int32 [16], P('shot'), may hold values from 0 to 262143
- wavelet: float32 [16, 12], P('shot'), may hold values from -12 to 12
- receiver_cell: int32 [16, 256], P('shot'), may hold values from 0 to 262143
- prev_row: int32 [16], replicated, may hold values from 0 to 15
- prev_grad: float32 [16, 32, 32, 256], P('shot', 'tile'), may hold values from -6 to 6
Outputs:
- final_state: float32 [16, 9, 32, 32, 256], P('shot', None, 'tile')
- image_sum: float32 [16, 32, 32, 256], P('shot', 'tile')
- owner_grad: float32 [512, 32, 256], P(('shot', 'tile'))
- traces: float32 [16, 12, 256], P('shot')
The draws below stay inside these ranges and needn't reach their ends.
Inputs may be any that keep to these rules, and one draw needn't show every extreme that they name: `aperture_row`: row q of model tiles holds the cells with x from q * 32 to q * 32 + 31; several shots may share a row and some rows have none. `prev_row`: rows of the previous batch, in the same sense. `source_cell`: flat index x * 32 * 256 + y * 256 + z within the shot's aperture. `receiver_cell`: flat indices as for source_cell; two receivers may share a cell.
All inputs are finite; a program needn't handle non-finite values.
Results may differ from the reference program's by a relative error of at most 0.0003.
Values sent between devices are 32-bit elements; how exact they have to be, the bound alone decides.
A program may use at most 64 MiB of HBM per device.

```python
import math
import jax
import jax.numpy as jnp
import numpy as np
from jax import lax

NY = 32
NZ = 256
NREC = 256
STEPS = 12
AX = 32
NX = 512
N_SHOT = 16


def touch_ends(drawn, key, smallest, high):
    longest = drawn.shape.index(max(drawn.shape))
    spots = []
    for shift in (0, 1):
        where = [jax.random.randint(jax.random.fold_in(key, axis), (), 0, length) for axis, length in enumerate(drawn.shape)]
        where[longest] = (where[longest] + shift) % drawn.shape[longest]
        spots.append(tuple(where))
    return drawn.at[spots[0]].set(smallest).at[spots[1]].set(high)


def block_scale(key, extent, shards, least, high):
    def one(axis_at, parts):
        steps = jax.random.uniform(jax.random.fold_in(jax.random.fold_in(key, 6), axis_at), (parts,), jnp.float32, least / len(shards), high / len(shards))
        return jnp.repeat(jnp.exp(steps), extent[axis_at] // parts).reshape((-1,) + (1,) * (len(extent) - axis_at - 1))

    gain = one(*shards[0])
    for cut in shards[1:]:
        gain = gain * one(*cut)
    return gain


def rank_table(number_of, slope):
    weights = [(1 << 20) // math.isqrt(rank ** slope) + 1 for rank in range(1, number_of + 1)]
    width = 1 + sum(weights) // (1 << 30)
    return np.cumsum(np.array([max(1, weight // width) for weight in weights]))


def skewed_ids(key, shape, number_of, lean):
    grid = rank_table(number_of, lean)
    lot = jax.random.randint(jax.random.fold_in(key, 1), shape, 0, int(grid[number_of - 1]))
    standing = jnp.searchsorted(jnp.asarray(grid, jnp.int32), lot, side="right")
    return jax.random.permutation(jax.random.fold_in(key, 2), number_of)[standing].astype(jnp.int32)


def bell_draw(rng, shape, spread, limit, pieces=(), kind=jnp.bfloat16):
    level = block_scale(rng, shape, pieces, -0.22, 0.18) if pieces else 1.0
    values = jax.random.normal(rng, shape, jnp.float32) * spread * level
    return jnp.minimum(jnp.maximum(values, -limit), limit).astype(kind)


def setup_inputs(seed: int = 0) -> dict:
    arg_keys = jax.random.split(jax.random.key(seed), 11)
    return {
        "lame_lambda": jnp.clip(1.0 + 1.0 * jax.random.uniform(arg_keys[0], (NX, NY, NZ), jnp.float32) ** block_scale(arg_keys[0], (NX, NY, NZ), ((0, 128),), -0.2, 0.2), 1.0, 2.0),
        "lame_mu": jnp.clip(0.5 + 0.5 * jax.random.uniform(arg_keys[1], (NX, NY, NZ), jnp.float32) ** block_scale(arg_keys[1], (NX, NY, NZ), ((0, 128),), -0.2, 0.2), 0.5, 1.0),
        "buoyancy": jnp.clip(0.5 + 0.5 * jax.random.uniform(arg_keys[2], (NX, NY, NZ), jnp.float32) ** block_scale(arg_keys[2], (NX, NY, NZ), ((0, 128),), -0.2, 0.2), 0.5, 1.0),
        "aperture_row": touch_ends(skewed_ids(arg_keys[3], (N_SHOT,), N_SHOT, 2), jax.random.fold_in(arg_keys[3], 3), 0, N_SHOT - 1).astype(jnp.int32),
        "wave_state": bell_draw(arg_keys[4], (N_SHOT, 9, AX, NY, NZ), 1.0, 6.0, ((0, 16), (2, 8)), jnp.float32),
        "source_cell": touch_ends(jax.random.randint(arg_keys[5], (N_SHOT,), 0, AX * NY * NZ), jax.random.fold_in(arg_keys[5], 1), 0, (AX * NY * NZ) - 1).astype(jnp.int32),
        "wavelet": bell_draw(arg_keys[6], (N_SHOT, STEPS), 2.0, 12.0, ((0, 16),), jnp.float32),
        "receiver_cell": touch_ends(jax.random.randint(arg_keys[7], (N_SHOT, NREC), 0, AX * NY * NZ), jax.random.fold_in(arg_keys[7], 1), 0, (AX * NY * NZ) - 1).astype(jnp.int32),
        "prev_row": touch_ends(skewed_ids(arg_keys[8], (N_SHOT,), N_SHOT, 2), jax.random.fold_in(arg_keys[8], 3), 0, N_SHOT - 1).astype(jnp.int32),
        "prev_grad": bell_draw(arg_keys[9], (N_SHOT, AX, NY, NZ), 1.0, 6.0, ((0, 16), (1, 8)), jnp.float32),
    }


coefficients = (0.8, -0.2, 4.0 / 105.0, -1.0 / 280.0)
time_step = 0.2


def central(padded, axis, length):
    result = None
    for neighbor in range(1, 5):
        forward = lax.slice_in_dim(padded, 4 + neighbor, 4 + neighbor + length, axis=axis)
        backward = lax.slice_in_dim(padded, 4 - neighbor, 4 - neighbor + length, axis=axis)
        term = coefficients[neighbor - 1] * (forward - backward)
        result = term if result is None else result + term
    return result


def derive(field, axis):
    widths = [(0, 0)] * field.ndim
    widths[axis] = (4, 4)
    return central(jnp.pad(field, widths), axis, field.shape[axis])


def pad_planes(stacked):
    return jnp.pad(stacked, ((0, 0), (4, 4), (0, 0), (0, 0)))


def inject(velocity_z, buoy_cells, where_local, amplitude):
    flat = velocity_z.reshape(-1)
    count = flat.shape[0]
    inside = (where_local >= 0) & (where_local < count)
    index_at = jnp.clip(where_local, 0, count - 1)
    added = jnp.where(inside, time_step * buoy_cells.reshape(-1)[index_at] * amplitude, 0.0)
    return flat.at[index_at].add(added).reshape(velocity_z.shape)


def sample_at(velocity_z, where_local):
    flat = velocity_z.reshape(-1)
    count = flat.shape[0]
    inside = (where_local >= 0) & (where_local < count)
    index_at = jnp.clip(where_local, 0, count - 1)
    return jnp.where(inside, flat[index_at], 0.0)


def advance_fields(fields, buoy_cells, lambda_cells, shear_cells, pad_stress, pad_velocity, source_local, amplitude):
    velocity_x, velocity_y, velocity_z, stress_xx, stress_yy, stress_zz, stress_xy, stress_xz, stress_yz = fields
    length = velocity_x.shape[0]
    stress_dx = central(pad_stress(jnp.stack([stress_xx, stress_xy, stress_xz])), 1, length)
    velocity_x = velocity_x + time_step * buoy_cells * (stress_dx[0] + derive(stress_xy, 1) + derive(stress_xz, 2))
    velocity_y = velocity_y + time_step * buoy_cells * (stress_dx[1] + derive(stress_yy, 1) + derive(stress_yz, 2))
    velocity_z = velocity_z + time_step * buoy_cells * (stress_dx[2] + derive(stress_yz, 1) + derive(stress_zz, 2))
    velocity_z = inject(velocity_z, buoy_cells, source_local, amplitude)
    velocity_dx = central(pad_velocity(jnp.stack([velocity_x, velocity_y, velocity_z])), 1, length)
    strain_xx = velocity_dx[0]
    strain_yy = derive(velocity_y, 1)
    strain_zz = derive(velocity_z, 2)
    dilation = strain_xx + strain_yy + strain_zz
    stress_xx = stress_xx + time_step * (lambda_cells * dilation + 2.0 * shear_cells * strain_xx)
    stress_yy = stress_yy + time_step * (lambda_cells * dilation + 2.0 * shear_cells * strain_yy)
    stress_zz = stress_zz + time_step * (lambda_cells * dilation + 2.0 * shear_cells * strain_zz)
    stress_xy = stress_xy + time_step * shear_cells * (derive(velocity_x, 1) + velocity_dx[1])
    stress_xz = stress_xz + time_step * shear_cells * (derive(velocity_x, 2) + velocity_dx[2])
    stress_yz = stress_yz + time_step * shear_cells * (derive(velocity_y, 2) + derive(velocity_z, 1))
    increment = dilation * (stress_xx + stress_yy + stress_zz)
    fields = (velocity_x, velocity_y, velocity_z, stress_xx, stress_yy, stress_zz, stress_xy, stress_xz, stress_yz)
    return fields, increment


def evolve(state, lambda_cells, shear_cells, buoy_cells, cell, pulses, receivers):
    fields = tuple(state[index] for index in range(9))

    def advance(carried, amplitude):
        fields, image_sum = carried
        fields, increment = advance_fields(fields, buoy_cells, lambda_cells, shear_cells, pad_planes, pad_planes, cell, amplitude)
        record = sample_at(fields[2], receivers)
        return (fields, image_sum + increment), record

    (fields, image_sum), records = lax.scan(advance, (fields, jnp.zeros_like(state[0])), pulses)
    return jnp.stack(fields), image_sum, records


def reference(lame_lambda, lame_mu, buoyancy, aperture_row, wave_state, source_cell, wavelet, receiver_cell, prev_row, prev_grad):
    def one_shot(shot_number):
        start_x = (aperture_row[shot_number] * AX).astype(jnp.int32)
        lambda_cells = lax.dynamic_slice_in_dim(lame_lambda, start_x, AX, 0)
        shear_cells = lax.dynamic_slice_in_dim(lame_mu, start_x, AX, 0)
        buoy_cells = lax.dynamic_slice_in_dim(buoyancy, start_x, AX, 0)
        return evolve(wave_state[shot_number], lambda_cells, shear_cells, buoy_cells,
                        source_cell[shot_number], wavelet[shot_number], receiver_cell[shot_number])

    final_state, image_sum, traces = lax.map(one_shot, jnp.arange(N_SHOT, dtype=jnp.int32))
    rows = jnp.arange(N_SHOT, dtype=jnp.int32)
    matches = (prev_row[None, :] == rows[:, None]).astype(jnp.float32)
    owner_grad = jnp.einsum("qs,sxyz->qxyz", matches, prev_grad.astype(jnp.float32), precision=lax.Precision.HIGHEST)
    owner_grad = owner_grad.reshape(NX, NY, NZ)
    return final_state, image_sum, owner_grad, traces
```

```python
import jax
import jax.numpy as jnp
import numpy as np
from jax import lax
from jax.experimental import pallas as pl
from jax.experimental.pallas import tpu as pltpu
from jax.sharding import PartitionSpec as P

MESH = pl.DeviceIdType.MESH
F32 = jnp.float32
BF16 = jnp.bfloat16

WEIGHTS = (672.0, -168.0, 32.0, -3.0)
UNIT = 1.0 / 840.0
DT = 0.2
STEPS = 12

STRESS = (5, 7, 8, 3, 4, 6)
SZZ, SXZ, SYZ, SXX, SYY, SXY = range(6)


def operators():
    gain = np.zeros(9)
    for k in range(1, 5):
        gain[4 + k] = WEIGHTS[k - 1]
        gain[4 - k] = -WEIGHTS[k - 1]

    def at(diff):
        return np.where(np.abs(diff) <= 4, gain[np.clip(diff, -4, 4) + 4], 0.0)

    lane = np.arange(128)
    x, y = lane // 32, lane % 32
    dx = x[:, None] - x[None, :]
    dy = y[:, None] - y[None, :]
    same_y = (dy == 0).astype(np.float64)
    same_x = (dx == 0).astype(np.float64)
    block = np.concatenate(
        [at(dx) * same_y, at(dx - 4) * same_y, at(dx + 4) * same_y, at(dy) * same_x], axis=1
    )
    return np.concatenate([block, block], axis=0)


def split(rows):
    hi = rows.astype(BF16)
    lo = (rows - hi.astype(F32)).astype(BF16)
    return jnp.concatenate([hi, lo], axis=1)


def kernel(
    ap_row, pr_row, wave, lam, mu, buoy, grad, params, weights,
    o_state, o_image, o_owner, o_trace,
    T, RW, TM, G, M, RM, GG, MO, PR, PRO,
    S, V, B, L, MU, MU2, SRC, IMG, R1, L2, TRB, TRS, TRR, OB, D2,
    w_send, w_recv, m_send, m_recv, n_send, n_recv, g_send, g_recv, h_send, h_recv,
    p_send, p_recv, halo_send, halo_recv, vb_send, vb_recv, t_send, t_recv, o_send, o_recv,
):
    s_i = lax.axis_index("shot")
    t_i = lax.axis_index("tile")
    core = s_i % 2
    base = s_i - core
    x_lo = t_i // 4
    y_i = t_i % 4
    role = base + x_lo
    d = 2 * y_i + core
    piece_d = s_i // 2
    half = s_i % 2
    swapped = core != x_lo
    not_self3 = piece_d != d

    barrier = pltpu.get_barrier_semaphore()

    def hello(shot, tile):
        pl.semaphore_signal(barrier, inc=1, device_id=(shot, tile), device_id_type=MESH)

    @pl.when(d == 0)
    def _():
        for par in range(2):
            S[par, :, 0:8] = jnp.zeros((6, 8, 8, 128), F32)
        V[:, 0:4] = jnp.zeros((3, 4, 8, 128), F32)
        B[0:4] = jnp.zeros((4, 8, 128), F32)

    @pl.when(d == 7)
    def _():
        for par in range(2):
            S[par, :, 40:48] = jnp.zeros((6, 8, 8, 128), F32)
        V[:, 36:40] = jnp.zeros((3, 4, 8, 128), F32)
        B[36:40] = jnp.zeros((4, 8, 128), F32)

    for k in range(1, 16):
        hello((s_i + k) % 16, t_i)
    for k in range(1, 8):
        for c in range(2):
            hello(base + c, (t_i + k) % 8)

    @pl.when(not_self3)
    def _():
        hello(2 * d + half, t_i)

    for k in range(8):
        for c in range(2):
            if k == 0 and c == 0:
                continue
            hello(2 * d + (half + c) % 2, (t_i + k) % 8)

    for m, ref in enumerate((lam, mu, buoy)):
        TM[m] = ref[...].T
    for f in range(9):
        T[f] = wave[f].T

    pl.semaphore_wait(barrier, 15 + 14 + 15 + not_self3.astype(jnp.int32))

    def spread_material(k):
        p = (s_i + k) % 16
        return pltpu.make_async_remote_copy(
            src_ref=TM.at[:, pl.ds(16 * p, 16), :],
            dst_ref=G.at[s_i],
            send_sem=m_send.at[k],
            recv_sem=m_recv,
            device_id=(p, t_i),
            device_id_type=MESH,
        )

    spread = [spread_material(k) for k in range(1, 16)]
    for copy in spread:
        copy.start()
    pltpu.make_async_copy(TM.at[:, pl.ds(16 * s_i, 16), :], G.at[s_i], m_recv).start()

    table = pltpu.make_async_remote_copy(
        src_ref=params,
        dst_ref=PRO,
        send_sem=p_send,
        recv_sem=p_recv,
        device_id=(base + 1 - core, t_i),
        device_id_type=MESH,
    )
    table.start()

    def move_wave(k):
        dd = (d + k) % 8
        return pltpu.make_async_remote_copy(
            src_ref=T.at[:, pl.ds(32 * dd, 32), :],
            dst_ref=RW.at[:, pl.ds(32 * t_i, 32), :],
            send_sem=w_send.at[k],
            recv_sem=w_recv,
            device_id=(base + dd % 2, core * 4 + dd // 2),
            device_id_type=MESH,
        )

    waves = [move_wave(k) for k in range(8)]
    for k in range(1, 8):
        waves[k].start()

    @pl.when(swapped)
    def _():
        waves[0].start()

    @pl.when(jnp.logical_not(swapped))
    def _():
        pltpu.make_async_copy(
            T.at[:, pl.ds(32 * d, 32), :], RW.at[:, pl.ds(32 * t_i, 32), :], w_recv
        ).start()

    def spread_grad(k):
        p = (s_i + k) % 16
        return pltpu.make_async_remote_copy(
            src_ref=grad.at[pl.ds(8 * p, 8), :],
            dst_ref=GG.at[s_i],
            send_sem=g_send.at[k],
            recv_sem=g_recv,
            device_id=(p, t_i),
            device_id_type=MESH,
        )

    grads = [spread_grad(k) for k in range(1, 16)]
    for copy in grads:
        copy.start()
    pltpu.make_async_copy(grad.at[pl.ds(8 * s_i, 8), :], GG.at[s_i], g_recv).start()

    pltpu.make_async_copy(G, G, m_recv).wait()
    for s in range(16):
        M[s] = G[ap_row[s]]

    def send_material(k):
        s = (role + k) % 16
        return pltpu.make_async_remote_copy(
            src_ref=M.at[s],
            dst_ref=RM.at[:, pl.ds(32 * t_i + 16 * half, 16), :],
            send_sem=n_send.at[k],
            recv_sem=n_recv,
            device_id=(s - s % 2 + piece_d % 2, (s % 2) * 4 + piece_d // 2),
            device_id_type=MESH,
        )

    deliver = [send_material(k) for k in range(16)]
    for k in range(1, 16):
        deliver[k].start()

    @pl.when(not_self3)
    def _():
        deliver[0].start()

    @pl.when(jnp.logical_not(not_self3))
    def _():
        pltpu.make_async_copy(
            M.at[role], RM.at[:, pl.ds(32 * t_i + 16 * half, 16), :], n_recv
        ).start()

    pltpu.make_async_copy(RW, RW, w_recv).wait()
    for z in range(32):
        for f in range(3):
            V[f, 4 + z] = RW[f, pl.ds(z, 8, stride=32), :]
        for j, f in enumerate(STRESS):
            S[0, j, 8 + z] = RW[f, pl.ds(z, 8, stride=32), :]

    left = jnp.maximum(d - 1, 0)
    right = jnp.minimum(d + 1, 7)
    left_id = (base + left % 2, x_lo * 4 + left // 2)
    right_id = (base + right % 2, x_lo * 4 + right // 2)

    def halo(par):
        def one(side, part, src, dst, device):
            return pltpu.make_async_remote_copy(
                src_ref=src,
                dst_ref=dst,
                send_sem=halo_send.at[par, side, part],
                recv_sem=halo_recv.at[par, side, part],
                device_id=device,
                device_id_type=MESH,
            )

        z3, o3 = pl.ds(0, 3), pl.ds(3, 3)
        to_left = [
            one(0, 0, S.at[par, z3, 8:16], S.at[par, z3, 40:48], left_id),
            one(0, 1, S.at[par, o3, 8:12], S.at[par, o3, 40:44], left_id),
        ]
        to_right = [
            one(1, 0, S.at[par, z3, 32:40], S.at[par, z3, 0:8], right_id),
            one(1, 1, S.at[par, o3, 36:40], S.at[par, o3, 4:8], right_id),
        ]
        return to_left, to_right

    has_left = d > 0
    has_right = d < 7

    def start_halo(par):
        to_left, to_right = halo(par)

        @pl.when(has_left)
        def _():
            for copy in to_left:
                copy.start()

        @pl.when(has_right)
        def _():
            for copy in to_right:
                copy.start()

    def wait_halo(par):
        to_left, to_right = halo(par)

        @pl.when(has_left)
        def _():
            for copy in to_left:
                copy.wait_send()
            for copy in to_right:
                copy.wait_recv()

        @pl.when(has_right)
        def _():
            for copy in to_right:
                copy.wait_send()
            for copy in to_left:
                copy.wait_recv()

    start_halo(0)

    pltpu.make_async_copy(RM, RM, n_recv).wait()
    for z in range(32):
        shear = RM[1, pl.ds(z, 8, stride=32), :] * (DT * UNIT)
        L[z] = RM[0, pl.ds(z, 8, stride=32), :] * (DT * UNIT)
        MU[z] = shear
        MU2[z] = 2.0 * shear
        B[4 + z] = RM[2, pl.ds(z, 8, stride=32), :]

    def vb(side, src_v, dst_v, src_b, dst_b, device):
        return [
            pltpu.make_async_remote_copy(
                src_ref=src, dst_ref=dst, send_sem=vb_send.at[side, i], recv_sem=vb_recv.at[side, i],
                device_id=device, device_id_type=MESH,
            )
            for i, (src, dst) in enumerate(((src_v, dst_v), (src_b, dst_b)))
        ]

    vb_left = vb(0, V.at[:, 4:8], V.at[:, 36:40], B.at[4:8], B.at[36:40], left_id)
    vb_right = vb(1, V.at[:, 32:36], V.at[:, 0:4], B.at[32:36], B.at[0:4], right_id)

    @pl.when(has_left)
    def _():
        for copy in vb_left:
            copy.start()

    @pl.when(has_right)
    def _():
        for copy in vb_right:
            copy.start()

    pltpu.make_async_copy(GG, GG, g_recv).wait()
    for q in range(16):
        total = jnp.zeros((8, 256), F32)
        for s in range(16):
            total = total + jnp.where(pr_row[s] == q, GG[s], 0.0)
        MO[q] = total

    def send_owner(k):
        q = (s_i + k) % 16
        return pltpu.make_async_remote_copy(
            src_ref=MO.at[q],
            dst_ref=o_owner.at[pl.ds(8 * s_i, 8), :],
            send_sem=h_send.at[k],
            recv_sem=h_recv,
            device_id=(q, t_i),
            device_id_type=MESH,
        )

    owners = [send_owner(k) for k in range(1, 16)]
    for copy in owners:
        copy.start()
    pltpu.make_async_copy(MO.at[s_i], o_owner.at[pl.ds(8 * s_i, 8), :], h_recv).start()

    table.wait()

    @pl.when(swapped)
    def _():
        PR[...] = PRO[...]

    @pl.when(jnp.logical_not(swapped))
    def _():
        PR[...] = params[...]

    for part in range(2):
        ids = jnp.broadcast_to(PR[16 + part : 17 + part, :], (128, 128)).T.astype(jnp.int32)
        z = ids & 255
        y = (ids >> 8) & 31
        x = ids >> 13
        mine = (z >> 5) == d
        row = (z & 31) * 8 + (x >> 2)
        lane = (x & 3) * 32 + y
        iota = lax.broadcasted_iota(jnp.int32, (128, 128), 1)
        rows = pl.ds(128 * part, 128)
        for j in range(2):
            hit = jnp.logical_and(mine, row == iota + 128 * j)
            R1[rows, 128 * j : 128 * j + 128] = jnp.where(hit, 1.0, 0.0).astype(BF16)
        here = jnp.where(lane == iota, 1.0, 0.0)
        L2[rows, 0:128] = here
        L2[rows, 128:256] = here

    @pl.when(has_left)
    def _():
        for copy in vb_left:
            copy.wait_send()
        for copy in vb_right:
            copy.wait_recv()

    @pl.when(has_right)
    def _():
        for copy in vb_right:
            copy.wait_send()
        for copy in vb_left:
            copy.wait_recv()

    sub = lax.broadcasted_iota(jnp.int32, (8, 128), 0)
    lane = lax.broadcasted_iota(jnp.int32, (8, 128), 1)
    cell = (4 * sub + lane // 32) * 8192 + (lane % 32) * 256 + (32 * d - 4)
    source = PR[18:19, :].astype(jnp.int32)
    for i in range(40):
        now = B[i]
        SRC[i] = jnp.where(cell + i == source, now * DT, 0.0)
        B[i] = now * (DT * UNIT)
    IMG[...] = jnp.zeros((32, 8, 128), F32)

    first = (sub == 0)[None]
    last = (sub == 7)[None]

    def flat(value):
        return value.reshape(64, 128)

    def along_x(same, before, after):
        down = jnp.where(first, 0.0, pltpu.roll(before.reshape(8, 8, 128), 1, 1))
        up = jnp.where(last, 0.0, pltpu.roll(after.reshape(8, 8, 128), 7, 1))
        return same.reshape(8, 8, 128) + (down + up)

    def along_z(load):
        total = None
        for k in range(1, 5):
            term = WEIGHTS[k - 1] * (load(k) - load(-k))
            total = term if total is None else total + term
        return total

    def velocity(par, i0, amplitude):
        def stress(j, shift=0):
            return S[par, j, pl.ds(i0 + 4 + shift, 8)]

        xs = jnp.concatenate([split(flat(stress(j))) for j in (SXX, SXY, SXZ)], axis=0)
        ys = jnp.concatenate([split(flat(stress(j))) for j in (SYY, SYZ)], axis=0)
        px = jnp.dot(xs, weights[...], preferred_element_type=F32)
        py = jnp.dot(ys, weights[:, 384:512], preferred_element_type=F32)

        def x_of(m):
            rows = px[64 * m : 64 * m + 64]
            return along_x(rows[:, 0:128], rows[:, 128:256], rows[:, 256:384])

        def y_of(rows):
            return rows.reshape(8, 8, 128)

        at = pl.ds(i0, 8)
        gain = B[at]
        V[0, at] = V[0, at] + gain * (
            x_of(0) + y_of(px[64:128, 384:512]) + along_z(lambda k: stress(SXZ, k))
        )
        V[1, at] = V[1, at] + gain * (
            x_of(1) + y_of(py[0:64]) + along_z(lambda k: stress(SYZ, k))
        )
        V[2, at] = (
            V[2, at]
            + gain * (x_of(2) + y_of(py[64:128]) + along_z(lambda k: stress(SZZ, k)))
            + SRC[at] * amplitude
        )

    def stresses(par, z0):
        def speed(j, shift=0):
            return V[j, pl.ds(z0 + 4 + shift, 8)]

        rows = jnp.concatenate([split(flat(speed(j))) for j in range(3)], axis=0)
        p = jnp.dot(rows, weights[...], preferred_element_type=F32)

        def x_of(m):
            r = p[64 * m : 64 * m + 64]
            return along_x(r[:, 0:128], r[:, 128:256], r[:, 256:384])

        def y_of(m):
            return p[64 * m : 64 * m + 64, 384:512].reshape(8, 8, 128)

        old = pl.ds(z0 + 8, 8)
        at = pl.ds(z0, 8)
        other = 1 - par
        shear = MU[at]
        exx = x_of(0)
        eyy = y_of(1)
        ezz = along_z(lambda k: speed(2, k))
        S[other, SXY, old] = S[par, SXY, old] + shear * (y_of(0) + x_of(1))
        S[other, SXZ, old] = S[par, SXZ, old] + shear * (along_z(lambda k: speed(0, k)) + x_of(2))
        S[other, SYZ, old] = S[par, SYZ, old] + shear * (along_z(lambda k: speed(1, k)) + y_of(2))
        div = exx + eyy + ezz
        bulk = L[at] * div
        twice = MU2[at]
        sxx = S[par, SXX, old] + (bulk + twice * exx)
        syy = S[par, SYY, old] + (bulk + twice * eyy)
        szz = S[par, SZZ, old] + (bulk + twice * ezz)
        S[other, SXX, old] = sxx
        S[other, SYY, old] = syy
        S[other, SZZ, old] = szz
        IMG[at] = IMG[at] + div * (sxx + syy + szz)

    def step(n, carry):
        par = lax.rem(n, 2)
        amplitude = PR[pl.ds(n, 1), :]
        for i0 in (8, 16, 24):
            velocity(par, i0, amplitude)
        wait_halo(par)
        for i0 in (0, 32):
            velocity(par, i0, amplitude)
        for z0 in (0, 24):
            stresses(par, z0)

        @pl.when(n < STEPS - 1)
        def _():
            start_halo(1 - par)

        for z0 in (8, 16):
            stresses(par, z0)
        picked = jnp.dot(R1[...], split(V[2, 4:36].reshape(256, 128)), preferred_element_type=F32)
        picked = (picked * L2[...]).astype(BF16)
        TRB[n] = lax.dot_general(
            jnp.ones((8, 256), BF16), picked, (((1,), (1,)), ((), ())), preferred_element_type=F32
        )
        return carry

    lax.fori_loop(0, STEPS, step, 0)

    for n in range(STEPS):
        TRS[n : n + 1, :] = TRB[n, 0:1, :]

    def home(k):
        t = (t_i + k) % 8
        return (base + x_lo, t)

    def send_trace(k):
        return pltpu.make_async_remote_copy(
            src_ref=TRS, dst_ref=TRR.at[d], send_sem=t_send.at[k], recv_sem=t_recv,
            device_id=home(k), device_id_type=MESH,
        )

    def send_home(k):
        t = (t_i + k) % 8
        return pltpu.make_async_remote_copy(
            src_ref=OB.at[:, pl.ds(32 * t, 32), :],
            dst_ref=D2.at[:, pl.ds(32 * d, 32), :],
            send_sem=o_send.at[k],
            recv_sem=o_recv,
            device_id=home(k),
            device_id_type=MESH,
        )

    traces = [send_trace(k) for k in range(8)]
    for k in range(1, 8):
        traces[k].start()

    for z in range(32):
        rows = pl.ds(z, 8, stride=32)
        for f in range(3):
            OB[f, rows, :] = V[f, 4 + z]
        for j, f in enumerate(STRESS):
            OB[f, rows, :] = S[0, j, 8 + z]
        OB[9, rows, :] = IMG[z] * UNIT

    homes = [send_home(k) for k in range(8)]
    for k in range(1, 8):
        homes[k].start()

    @pl.when(swapped)
    def _():
        traces[0].start()
        homes[0].start()

    @pl.when(jnp.logical_not(swapped))
    def _():
        pltpu.make_async_copy(TRS, TRR.at[d], t_recv).start()
        pltpu.make_async_copy(
            OB.at[:, pl.ds(32 * t_i, 32), :], D2.at[:, pl.ds(32 * d, 32), :], o_recv
        ).start()

    for copies in (spread, grads, owners):
        for copy in copies:
            copy.wait_send()
    for k in range(1, 8):
        waves[k].wait_send()
    for k in range(1, 16):
        deliver[k].wait_send()

    @pl.when(swapped)
    def _():
        waves[0].wait_send()

    @pl.when(not_self3)
    def _():
        deliver[0].wait_send()

    pltpu.make_async_copy(o_owner, o_owner, h_recv).wait()

    pltpu.make_async_copy(TRR, TRR, t_recv).wait()
    total = TRR[0]
    for j in range(1, 8):
        total = total + TRR[j]
    o_trace[...] = total

    pltpu.make_async_copy(D2, D2, o_recv).wait()
    for f in range(9):
        o_state[f] = D2[f].T
    o_image[...] = D2[9].T

    for k in range(1, 8):
        traces[k].wait_send()
        homes[k].wait_send()

    @pl.when(swapped)
    def _():
        traces[0].wait_send()
        homes[0].wait_send()


def on_device(
    lame_lambda, lame_mu, buoyancy, aperture_row, wave_state, source_cell, wavelet, receiver_cell,
    prev_row, prev_grad,
):
    rows = jnp.broadcast_to(wavelet[0][:, None], (STEPS, 128))
    params = jnp.concatenate(
        [
            rows,
            jnp.zeros((4, 128), F32),
            receiver_cell[0].reshape(2, 128).astype(F32),
            jnp.broadcast_to(source_cell.astype(F32)[:, None], (1, 128)),
            jnp.zeros((5, 128), F32),
        ],
        axis=0,
    )
    weights = jnp.asarray(operators(), BF16)
    vmem = pl.BlockSpec(memory_space=pltpu.VMEM)
    smem = pl.BlockSpec(memory_space=pltpu.SMEM)
    dma = pltpu.SemaphoreType.DMA
    planes = (8, 128)
    state, image, owner, trace = pl.pallas_call(
        kernel,
        out_shape=(
            jax.ShapeDtypeStruct((9, 128, 256), F32),
            jax.ShapeDtypeStruct((128, 256), F32),
            jax.ShapeDtypeStruct((128, 256), F32),
            jax.ShapeDtypeStruct((STEPS, 256), F32),
        ),
        in_specs=[smem, smem] + [vmem] * 7,
        out_specs=(vmem, vmem, vmem, vmem),
        scratch_shapes=[
            pltpu.VMEM((9, 256, 128), F32),
            pltpu.VMEM((9, 256, 128), F32),
            pltpu.VMEM((3, 256, 128), F32),
            pltpu.VMEM((16, 3, 16, 128), F32),
            pltpu.VMEM((16, 3, 16, 128), F32),
            pltpu.VMEM((3, 256, 128), F32),
            pltpu.VMEM((16, 8, 256), F32),
            pltpu.VMEM((16, 8, 256), F32),
            pltpu.VMEM((24, 128), F32),
            pltpu.VMEM((24, 128), F32),
            pltpu.VMEM((2, 6, 48) + planes, F32),
            pltpu.VMEM((3, 40) + planes, F32),
            pltpu.VMEM((40,) + planes, F32),
            pltpu.VMEM((32,) + planes, F32),
            pltpu.VMEM((32,) + planes, F32),
            pltpu.VMEM((32,) + planes, F32),
            pltpu.VMEM((40,) + planes, F32),
            pltpu.VMEM((32,) + planes, F32),
            pltpu.VMEM((256, 256), BF16),
            pltpu.VMEM((256, 256), F32),
            pltpu.VMEM((STEPS, 8, 256), F32),
            pltpu.VMEM((STEPS, 256), F32),
            pltpu.VMEM((8, STEPS, 256), F32),
            pltpu.VMEM((10, 256, 128), F32),
            pltpu.VMEM((10, 256, 128), F32),
            dma((8,)), dma, dma((16,)), dma, dma((16,)), dma, dma((16,)), dma, dma((16,)), dma,
            dma, dma, dma((2, 2, 2)), dma((2, 2, 2)), dma((2, 2)), dma((2, 2)),
            dma((8,)), dma, dma((8,)), dma,
        ],
        compiler_params=pltpu.CompilerParams(collective_id=0, has_side_effects=True),
        name="wave",
    )(
        aperture_row,
        prev_row,
        wave_state.reshape(9, 128, 256),
        lame_lambda.reshape(128, 256),
        lame_mu.reshape(128, 256),
        buoyancy.reshape(128, 256),
        prev_grad.reshape(128, 256),
        params,
        weights,
    )
    return (
        state.reshape(1, 9, 4, 32, 256),
        image.reshape(1, 4, 32, 256),
        owner.reshape(4, 32, 256),
        trace[None],
    )


def solution(mesh):
    placed = (
        P(("shot", "tile"), None, None),
        P(("shot", "tile"), None, None),
        P(("shot", "tile"), None, None),
        P(),
        P("shot", None, "tile", None, None),
        P("shot"),
        P("shot", None),
        P("shot", None),
        P(),
        P("shot", "tile", None, None),
    )
    return jax.shard_map(
        on_device,
        mesh=mesh,
        in_specs=placed,
        out_specs=(
            P("shot", None, "tile", None, None),
            P("shot", "tile", None, None),
            P(("shot", "tile"), None, None),
            P("shot", None, None),
        ),
        check_vma=False,
    )
```

```python
import jax
import jax.numpy as jnp
import numpy as np
from jax import lax
from jax.experimental import pallas as pl
from jax.experimental.pallas import tpu as pltpu
from jax.sharding import PartitionSpec as P

MESH = pl.DeviceIdType.MESH
F32 = jnp.float32
BF16 = jnp.bfloat16

WEIGHTS = (672.0, -168.0, 32.0, -3.0)
UNIT = 1.0 / 840.0
DT = 0.2
STEPS = 12

WAVE_ORDER = (4, 3, 5, 2, 6, 1, 7)

VELOCITY = (0, 1, 2)
WITH_Z = (7, 8, 5)
IN_PLANE = (3, 4, 6)


def operators():
    gain = np.zeros(9)
    for k in range(1, 5):
        gain[4 + k] = WEIGHTS[k - 1]
        gain[4 - k] = -WEIGHTS[k - 1]

    def at(diff):
        return np.where(np.abs(diff) <= 4, gain[np.clip(diff, -4, 4) + 4], 0.0)

    lane = np.arange(128)
    x, y = lane // 32, lane % 32
    dx = x[:, None] - x[None, :]
    dy = y[:, None] - y[None, :]
    same_y = (dy == 0).astype(np.float64)
    same_x = (dx == 0).astype(np.float64)
    block = np.concatenate(
        [at(dx) * same_y, at(dx - 4) * same_y, at(dx + 4) * same_y, at(dy) * same_x], axis=1
    )
    return np.concatenate([block, block], axis=0)


def split(rows):
    hi = rows.astype(BF16)
    lo = (rows - hi.astype(F32)).astype(BF16)
    return jnp.concatenate([hi, lo], axis=1)


def kernel(
    ap_row, pr_row, source, wavelet, receivers, wave, lam, mu, buoy, grad, weights,
    o_planes, o_owner, o_trace,
    T, RW, TM, G, M, RM, GG, MO,
    SZ, SO, V, B, L, MU, MU2, SRC, IMG, HR, QB, QR, R1, L2, TRB, TRS, TRR, OB,
    w_send, w_recv, m_send, m_recv, n_send, n_recv, g_send, g_recv, h_send, h_recv,
    halo_send, halo_recv, b_send, b_recv, t_send, t_recv, o_send, o_recv,
):
    s_i = lax.axis_index("shot")
    t_i = lax.axis_index("tile")

    def snake(i):
        return jnp.where(i < 4, i, 11 - i)

    d = snake(t_i)
    piece_d = s_i // 2
    half = s_i % 2
    elsewhere = piece_d != d
    has_left = d > 0
    has_right = d < 7
    left_id = (s_i, snake(jnp.maximum(d - 1, 0)))
    right_id = (s_i, snake(jnp.minimum(d + 1, 7)))

    def remote(src, dst, send, recv, device):
        return pltpu.make_async_remote_copy(
            src_ref=src, dst_ref=dst, send_sem=send, recv_sem=recv, device_id=device, device_id_type=MESH
        )

    barrier = pltpu.get_barrier_semaphore()

    def hello(shot, tile):
        pl.semaphore_signal(barrier, inc=1, device_id=(shot, tile), device_id_type=MESH)

    for k in range(1, 16):
        hello((s_i + k) % 16, t_i)
    for k in range(1, 8):
        hello(s_i, (t_i + k) % 8)

    @pl.when(elsewhere)
    def _():
        hello(2 * d + half, t_i)

    for k in range(8):
        for c in range(2):
            if k + c:
                hello(2 * d + (half + c) % 2, (t_i + k) % 8)

    for m, ref in enumerate((lam, mu, buoy)):
        TM[m] = ref[...].T
    for f in range(9):
        T[f] = wave[f].T

    SZ[:, 0:4] = jnp.zeros((3, 4, 8, 128), F32)
    SZ[:, 36:40] = jnp.zeros((3, 4, 8, 128), F32)

    def blank(side):
        for par in range(2):
            HR[par, side] = jnp.zeros((3, 4, 8, 128), F32)
            QR[par, side] = jnp.zeros((3, 4, 8, 128), F32)
        B[36 * side : 36 * side + 4] = jnp.zeros((4, 8, 128), F32)

    pl.when(jnp.logical_not(has_left))(lambda: blank(0))
    pl.when(jnp.logical_not(has_right))(lambda: blank(1))

    pl.semaphore_wait(barrier, 15 + 7 + 15 + elsewhere.astype(jnp.int32))

    def spread_material(k):
        p = (s_i + k) % 16
        return remote(TM.at[:, pl.ds(16 * p, 16), :], G.at[s_i], m_send.at[k], m_recv, (p, t_i))

    spread = [spread_material(k) for k in range(1, 16)]
    for copy in spread:
        copy.start()
    pltpu.make_async_copy(TM.at[:, pl.ds(16 * s_i, 16), :], G.at[s_i], m_recv).start()

    def move_wave(k):
        dd = (d + k) % 8
        return remote(
            T.at[:, pl.ds(32 * dd, 32), :],
            RW.at[:, pl.ds(32 * t_i, 32), :],
            w_send.at[k],
            w_recv,
            (s_i, snake(dd)),
        )

    waves = [move_wave(k) for k in WAVE_ORDER]
    for copy in waves:
        copy.start()
    pltpu.make_async_copy(T.at[:, pl.ds(32 * d, 32), :], RW.at[:, pl.ds(32 * t_i, 32), :], w_recv).start()

    iota = lax.broadcasted_iota(jnp.int32, (128, 128), 1)
    for part in range(2):
        ids = jnp.broadcast_to(receivers[:, 128 * part : 128 * part + 128], (128, 128)).astype(F32)
        ids = ids.T.astype(jnp.int32)
        z = ids & 255
        y = (ids >> 8) & 31
        x = ids >> 13
        mine = (z >> 5) == d
        row = (z & 31) * 8 + (x >> 2)
        lane = (x & 3) * 32 + y
        rows = pl.ds(128 * part, 128)
        for j in range(2):
            hit = jnp.logical_and(mine, row == iota + 128 * j)
            R1[rows, 128 * j : 128 * j + 128] = jnp.where(hit, 1.0, 0.0).astype(BF16)
        here = jnp.where(lane == iota, 1.0, 0.0)
        L2[rows, 0:128] = here
        L2[rows, 128:256] = here
    IMG[...] = jnp.zeros((32, 8, 128), F32)

    pltpu.make_async_copy(G, G, m_recv).wait()
    for s in range(16):
        M[s] = G[ap_row[s]]

    def send_material(k):
        s = (s_i + k) % 16
        return remote(
            M.at[s],
            RM.at[:, pl.ds(32 * t_i + 16 * half, 16), :],
            n_send.at[k],
            n_recv,
            (s, snake(piece_d)),
        )

    deliver = [send_material(k) for k in range(16)]
    for k in range(1, 16):
        deliver[k].start()

    @pl.when(elsewhere)
    def _():
        deliver[0].start()

    @pl.when(jnp.logical_not(elsewhere))
    def _():
        pltpu.make_async_copy(M.at[s_i], RM.at[:, pl.ds(32 * t_i + 16 * half, 16), :], n_recv).start()

    def spread_grad(k):
        p = (s_i + k) % 16
        return remote(grad.at[pl.ds(8 * p, 8), :], GG.at[s_i], g_send.at[k], g_recv, (p, t_i))

    grads = [spread_grad(k) for k in range(1, 16)]
    for copy in grads:
        copy.start()
    pltpu.make_async_copy(grad.at[pl.ds(8 * s_i, 8), :], GG.at[s_i], g_recv).start()

    pltpu.make_async_copy(RW, RW, w_recv).wait()
    for z in range(32):
        rows = pl.ds(z, 8, stride=32)
        for j, f in enumerate(WITH_Z):
            SZ[j, 4 + z] = RW[f, rows, :]
        for j, f in enumerate(IN_PLANE):
            SO[j, z] = RW[f, rows, :]
        for j, f in enumerate(VELOCITY):
            V[j, 4 + z] = RW[f, rows, :]

    def halo(par, part):
        def one(side, src, dst, device):
            return remote(src, dst, halo_send.at[par, side, part], halo_recv.at[par, side, part], device)

        if part == 0:
            to_left = one(0, SZ.at[:, 4:8], HR.at[par, 1], left_id)
            to_right = one(1, SZ.at[:, 32:36], HR.at[par, 0], right_id)
        else:
            to_left = one(0, QB.at[par, 0], QR.at[par, 1], left_id)
            to_right = one(1, QB.at[par, 1], QR.at[par, 0], right_id)
        return to_left, to_right

    def start_halo(par, part):
        to_left, to_right = halo(par, part)
        pl.when(has_left)(to_left.start)
        pl.when(has_right)(to_right.start)

    def wait_halo(par):
        for part in range(2):
            to_left, to_right = halo(par, part)

            @pl.when(has_left)
            def _():
                to_left.wait_send()
                to_right.wait_recv()

            @pl.when(has_right)
            def _():
                to_right.wait_send()
                to_left.wait_recv()

    start_halo(0, 0)

    pltpu.make_async_copy(RM, RM, n_recv).wait()
    for z in range(32):
        B[4 + z] = RM[2, pl.ds(z, 8, stride=32), :] * (DT * UNIT)

    b_left = remote(B.at[4:8], B.at[36:40], b_send.at[0], b_recv.at[0], left_id)
    b_right = remote(B.at[32:36], B.at[0:4], b_send.at[1], b_recv.at[1], right_id)
    pl.when(has_left)(b_left.start)
    pl.when(has_right)(b_right.start)

    sub = lax.broadcasted_iota(jnp.int32, (8, 128), 0)
    lane = lax.broadcasted_iota(jnp.int32, (8, 128), 1)
    cell = (4 * sub + lane // 32) * 8192 + (lane % 32) * 256 + 32 * d
    where_source = source[0]
    for z in range(32):
        shear = RM[1, pl.ds(z, 8, stride=32), :] * (DT * UNIT)
        L[z] = RM[0, pl.ds(z, 8, stride=32), :] * (DT * UNIT)
        MU[z] = shear
        MU2[z] = 2.0 * shear
        SRC[z] = jnp.where(cell + z == where_source, RM[2, pl.ds(z, 8, stride=32), :] * DT, 0.0)

    first = (sub == 0)[None]
    last = (sub == 7)[None]

    def flat(value):
        return value.reshape(64, 128)

    def along_x(same, before, after):
        down = jnp.where(first, 0.0, pltpu.roll(before.reshape(8, 8, 128), 1, 1))
        up = jnp.where(last, 0.0, pltpu.roll(after.reshape(8, 8, 128), 7, 1))
        return same.reshape(8, 8, 128) + (down + up)

    def along_z(load):
        total = None
        for k in range(1, 5):
            term = WEIGHTS[k - 1] * (load(k) - load(-k))
            total = term if total is None else total + term
        return total

    def velocity(parts, amplitude):
        def take(ref, *index, shift=0):
            got = [ref[index + (pl.ds(z + shift, n),)] for z, n in parts]
            return got[0] if len(got) == 1 else jnp.concatenate(got, axis=0)

        def with_z(j, shift=0):
            return take(SZ, j, shift=4 + shift)

        fields = (take(SO, 0), take(SO, 2), with_z(0), take(SO, 1), with_z(1))
        xs = jnp.concatenate([split(flat(field)) for field in fields[0:3]], axis=0)
        ys = jnp.concatenate([split(flat(field)) for field in fields[3:5]], axis=0)
        px = jnp.dot(xs, weights[...], preferred_element_type=F32)
        py = jnp.dot(ys, weights[:, 384:512], preferred_element_type=F32)

        def x_of(m):
            rows = px[64 * m : 64 * m + 64]
            return along_x(rows[:, 0:128], rows[:, 128:256], rows[:, 256:384])

        def y_of(rows):
            return rows.reshape(8, 8, 128)

        ys = (y_of(px[64:128, 384:512]), y_of(py[0:64]), y_of(py[64:128]))
        gain = take(B, shift=4)
        new = [
            take(V, j, shift=4) + gain * (x_of(j) + ys[j] + along_z(lambda k: with_z(j, k)))
            for j in range(3)
        ]
        new[2] = new[2] + take(SRC) * amplitude
        return new

    def inner_velocity(z0, amplitude):
        new = velocity([(z0, 8)], amplitude)
        for j in range(3):
            V[j, pl.ds(z0 + 4, 8)] = new[j]

    def partial_velocity(par, amplitude):
        new = velocity([(0, 4), (28, 4)], amplitude)
        for j in range(3):
            QB[par, 0, j] = new[j][0:4]
            QB[par, 1, j] = new[j][4:8]

    def complete_velocity(par):
        for j in range(4):
            low = high = None
            for k in range(j + 1, 5):
                term = WEIGHTS[k - 1] * HR[par, 0, :, 4 + j - k]
                low = term if low is None else low + term
            for k in range(4 - j, 5):
                term = WEIGHTS[k - 1] * HR[par, 1, :, j - 4 + k]
                high = term if high is None else high + term
            V[:, 4 + j] = QB[par, 0, :, j] - B[4 + j] * low
            V[:, 32 + j] = QB[par, 1, :, j] + B[32 + j] * high
            low = high = None
            for k in range(4 - j, 5):
                term = WEIGHTS[k - 1] * SZ[:, j + k]
                low = term if low is None else low + term
            for k in range(j + 1, 5):
                term = WEIGHTS[k - 1] * SZ[:, 36 + j - k]
                high = term if high is None else high + term
            V[:, j] = QR[par, 0, :, j] + B[j] * low
            V[:, 36 + j] = QR[par, 1, :, j] - B[36 + j] * high

    def stresses(z0):
        def speed(j, shift=0):
            return V[j, pl.ds(z0 + 4 + shift, 8)]

        rows = jnp.concatenate([split(flat(speed(j))) for j in range(3)], axis=0)
        p = jnp.dot(rows, weights[...], preferred_element_type=F32)

        def x_of(m):
            r = p[64 * m : 64 * m + 64]
            return along_x(r[:, 0:128], r[:, 128:256], r[:, 256:384])

        def y_of(m):
            return p[64 * m : 64 * m + 64, 384:512].reshape(8, 8, 128)

        at = pl.ds(z0, 8)
        wide = pl.ds(z0 + 4, 8)
        shear = MU[at]
        exx = x_of(0)
        eyy = y_of(1)
        ezz = along_z(lambda k: speed(2, k))
        SZ[0, wide] = SZ[0, wide] + shear * (along_z(lambda k: speed(0, k)) + x_of(2))
        SZ[1, wide] = SZ[1, wide] + shear * (along_z(lambda k: speed(1, k)) + y_of(2))
        SO[2, at] = SO[2, at] + shear * (y_of(0) + x_of(1))
        div = exx + eyy + ezz
        bulk = L[at] * div
        twice = MU2[at]
        szz = SZ[2, wide] + (bulk + twice * ezz)
        sxx = SO[0, at] + (bulk + twice * exx)
        syy = SO[1, at] + (bulk + twice * eyy)
        SZ[2, wide] = szz
        SO[0, at] = sxx
        SO[1, at] = syy
        IMG[at] = IMG[at] + div * (sxx + syy + szz)

    def send_owner(k):
        q = (s_i + k) % 16
        return remote(MO.at[q], o_owner.at[pl.ds(8 * s_i, 8), :], h_send.at[k], h_recv, (q, t_i))

    owners = [send_owner(k) for k in range(1, 16)]

    def gradients():
        pltpu.make_async_copy(GG, GG, g_recv).wait()
        for q in range(16):
            total = jnp.zeros((8, 256), F32)
            for s in range(16):
                total = total + jnp.where(pr_row[s] == q, GG[s], 0.0)
            MO[q] = total
        for copy in owners:
            copy.start()
        pltpu.make_async_copy(MO.at[s_i], o_owner.at[pl.ds(8 * s_i, 8), :], h_recv).start()

    partial_velocity(0, wavelet[0, 0])
    start_halo(0, 1)

    @pl.when(has_left)
    def _():
        b_left.wait_send()
        b_right.wait_recv()

    @pl.when(has_right)
    def _():
        b_right.wait_send()
        b_left.wait_recv()

    def step(n, carry):
        par = lax.rem(n, 2)
        amplitude = wavelet[0, n]
        for z0 in (4, 12, 20):
            inner_velocity(z0, amplitude)
        wait_halo(par)
        complete_velocity(par)
        for z0 in (0, 24):
            stresses(z0)

        @pl.when(n < STEPS - 1)
        def _():
            start_halo(1 - par, 0)
            partial_velocity(1 - par, wavelet[0, jnp.minimum(n + 1, STEPS - 1)])
            start_halo(1 - par, 1)

        for z0 in (8, 16):
            stresses(z0)
        picked = jnp.dot(R1[...], split(V[2, 4:36].reshape(256, 128)), preferred_element_type=F32)
        picked = (picked * L2[...]).astype(BF16)
        TRB[n] = lax.dot_general(
            jnp.ones((8, 256), BF16), picked, (((1,), (1,)), ((), ())), preferred_element_type=F32
        )
        pl.when(n == 1)(gradients)
        return carry

    lax.fori_loop(0, STEPS, step, 0)

    for z in range(32):
        rows = pl.ds(z, 8, stride=32)
        for j, f in enumerate(VELOCITY):
            OB[f, rows, :] = V[j, 4 + z]
        for j, f in enumerate(WITH_Z):
            OB[f, rows, :] = SZ[j, 4 + z]
        for j, f in enumerate(IN_PLANE):
            OB[f, rows, :] = SO[j, z]
        OB[9, rows, :] = IMG[z] * UNIT

    def send_home(k):
        t = snake((d + k) % 8)
        return remote(
            OB.at[:, pl.ds(32 * t, 32), :],
            o_planes.at[:, pl.ds(32 * d, 32), :],
            o_send.at[k],
            o_recv,
            (s_i, t),
        )

    homes = [send_home(k) for k in WAVE_ORDER]
    for copy in homes:
        copy.start()
    pltpu.make_async_copy(
        OB.at[:, pl.ds(32 * t_i, 32), :], o_planes.at[:, pl.ds(32 * d, 32), :], o_recv
    ).start()

    for n in range(STEPS):
        TRS[n : n + 1, :] = TRB[n, 0:1, :]

    def send_trace(k):
        return remote(TRS, TRR.at[d], t_send.at[k], t_recv, (s_i, snake((d + k) % 8)))

    traces = [send_trace(k) for k in range(1, 8)]
    for copy in traces:
        copy.start()
    pltpu.make_async_copy(TRS, TRR.at[d], t_recv).start()

    for copies in (spread, grads, owners, waves):
        for copy in copies:
            copy.wait_send()
    for k in range(1, 16):
        deliver[k].wait_send()
    pl.when(elsewhere)(deliver[0].wait_send)
    pltpu.make_async_copy(o_owner, o_owner, h_recv).wait()

    pltpu.make_async_copy(TRR, TRR, t_recv).wait()
    total = TRR[0]
    for j in range(1, 8):
        total = total + TRR[j]
    o_trace[...] = total

    pltpu.make_async_copy(o_planes, o_planes, o_recv).wait()
    for copy in homes + traces:
        copy.wait_send()


def finish(planes, owner, trace, o_state, o_image, o_owner, o_trace):
    for f in range(9):
        o_state[f] = planes[f].T
    o_image[...] = planes[9].T
    o_owner[...] = owner[...]
    o_trace[...] = trace[...]


def on_device(
    lame_lambda, lame_mu, buoyancy, aperture_row, wave_state, source_cell, wavelet, receiver_cell,
    prev_row, prev_grad,
):
    weights = jnp.asarray(operators(), BF16)
    vmem = pl.BlockSpec(memory_space=pltpu.VMEM)
    smem = pl.BlockSpec(memory_space=pltpu.SMEM)
    dma = pltpu.SemaphoreType.DMA
    tile = (8, 128)
    planes, owner, trace = pl.pallas_call(
        kernel,
        out_shape=(
            jax.ShapeDtypeStruct((10, 256, 128), F32),
            jax.ShapeDtypeStruct((128, 256), F32),
            jax.ShapeDtypeStruct((STEPS, 256), F32),
        ),
        in_specs=[smem] * 4 + [vmem] * 7,
        out_specs=(pl.BlockSpec(memory_space=pl.ANY), vmem, vmem),
        scratch_shapes=[
            pltpu.VMEM((9, 256, 128), F32),
            pltpu.VMEM((9, 256, 128), F32),
            pltpu.VMEM((3, 256, 128), F32),
            pltpu.VMEM((16, 3, 16, 128), F32),
            pltpu.VMEM((16, 3, 16, 128), F32),
            pltpu.VMEM((3, 256, 128), F32),
            pltpu.VMEM((16, 8, 256), F32),
            pltpu.VMEM((16, 8, 256), F32),
            pltpu.VMEM((3, 40) + tile, F32),
            pltpu.VMEM((3, 32) + tile, F32),
            pltpu.VMEM((3, 40) + tile, F32),
            pltpu.VMEM((40,) + tile, F32),
            pltpu.VMEM((32,) + tile, F32),
            pltpu.VMEM((32,) + tile, F32),
            pltpu.VMEM((32,) + tile, F32),
            pltpu.VMEM((32,) + tile, F32),
            pltpu.VMEM((32,) + tile, F32),
            pltpu.VMEM((2, 2, 3, 4) + tile, F32),
            pltpu.VMEM((2, 2, 3, 4) + tile, F32),
            pltpu.VMEM((2, 2, 3, 4) + tile, F32),
            pltpu.VMEM((256, 256), BF16),
            pltpu.VMEM((256, 256), F32),
            pltpu.VMEM((STEPS, 8, 256), F32),
            pltpu.VMEM((STEPS, 256), F32),
            pltpu.VMEM((8, STEPS, 256), F32),
            pltpu.VMEM((10, 256, 128), F32),
            dma((8,)), dma, dma((16,)), dma, dma((16,)), dma, dma((16,)), dma, dma((16,)), dma,
            dma((2, 2, 2)), dma((2, 2, 2)), dma((2,)), dma((2,)), dma((8,)), dma, dma((8,)), dma,
        ],
        compiler_params=pltpu.CompilerParams(collective_id=0, has_side_effects=True),
        name="wave",
    )(
        aperture_row,
        prev_row,
        source_cell,
        wavelet,
        receiver_cell,
        wave_state.reshape(9, 128, 256),
        lame_lambda.reshape(128, 256),
        lame_mu.reshape(128, 256),
        buoyancy.reshape(128, 256),
        prev_grad.reshape(128, 256),
        weights,
    )
    state, image, owner, trace = pl.pallas_call(
        finish,
        out_shape=(
            jax.ShapeDtypeStruct((9, 128, 256), F32),
            jax.ShapeDtypeStruct((128, 256), F32),
            jax.ShapeDtypeStruct((128, 256), F32),
            jax.ShapeDtypeStruct((STEPS, 256), F32),
        ),
        in_specs=[vmem] * 3,
        out_specs=(vmem,) * 4,
        name="finish",
    )(planes, owner, trace)
    return (
        state.reshape(1, 9, 4, 32, 256),
        image.reshape(1, 4, 32, 256),
        owner.reshape(4, 32, 256),
        trace[None],
    )


def solution(mesh):
    placed = (
        P(("shot", "tile"), None, None),
        P(("shot", "tile"), None, None),
        P(("shot", "tile"), None, None),
        P(),
        P("shot", None, "tile", None, None),
        P("shot"),
        P("shot", None),
        P("shot", None),
        P(),
        P("shot", "tile", None, None),
    )
    return jax.shard_map(
        on_device,
        mesh=mesh,
        in_specs=placed,
        out_specs=(
            P("shot", None, "tile", None, None),
            P("shot", "tile", None, None),
            P(("shot", "tile"), None, None),
            P("shot", None, None),
        ),
        check_vma=False,
    )
```

```python
import jax
import jax.numpy as jnp
import numpy as np
from jax import lax
from jax.experimental import pallas as pl
from jax.experimental.pallas import tpu as pltpu
from jax.sharding import PartitionSpec as P

MESH = pl.DeviceIdType.MESH
F32 = jnp.float32
BF16 = jnp.bfloat16

WEIGHTS = (672.0, -168.0, 32.0, -3.0)
UNIT = 1.0 / 840.0
DT = 0.2
STEPS = 12

WAVE_ORDER = (1, 3, 2, 4, 5, 7, 6)

VELOCITY = (0, 1, 2)
WITH_Z = (7, 8, 5)
IN_PLANE = (3, 4, 6)


def operators():
    gain = np.zeros(9)
    for k in range(1, 5):
        gain[4 + k] = WEIGHTS[k - 1]
        gain[4 - k] = -WEIGHTS[k - 1]

    def at(diff):
        return np.where(np.abs(diff) <= 4, gain[np.clip(diff, -4, 4) + 4], 0.0)

    lane = np.arange(128)
    x, y = lane // 32, lane % 32
    dx = x[:, None] - x[None, :]
    dy = y[:, None] - y[None, :]
    same_y = (dy == 0).astype(np.float64)
    same_x = (dx == 0).astype(np.float64)
    block = np.concatenate(
        [at(dx) * same_y, at(dx - 4) * same_y, at(dx + 4) * same_y, at(dy) * same_x], axis=1
    )
    return np.concatenate([block, block], axis=0)


def split(rows):
    hi = rows.astype(BF16)
    lo = (rows - hi.astype(F32)).astype(BF16)
    return jnp.concatenate([hi, lo], axis=1)


def kernel(
    ap_row, pr_row, source, wavelet, receivers, wave, lam, mu, buoy, grad, weights,
    o_planes, o_owner, o_trace,
    T, RW, TM, G, M, RM, GG, MO,
    SZ, SO, V, B, L, MU, MU2, SRC, IMG, HR, QB, QR, R1, L2, TRB, TRS, TRR, OB,
    w_send, w_recv, m_send, m_recv, n_send, n_recv, g_send, g_recv, h_send, h_recv,
    halo_send, halo_recv, b_send, b_recv, t_send, t_recv, o_send, o_recv,
):
    s_i = lax.axis_index("shot")
    t_i = lax.axis_index("tile")

    def snake(i):
        return jnp.where(i < 4, i, 11 - i)

    d = snake(t_i)
    piece = (s_i + 2 * t_i) % 16
    piece_d = piece // 2
    half = piece % 2
    elsewhere = piece_d != d
    has_left = d > 0
    has_right = d < 7
    left_id = (s_i, snake(jnp.maximum(d - 1, 0)))
    right_id = (s_i, snake(jnp.minimum(d + 1, 7)))

    def remote(src, dst, send, recv, device):
        return pltpu.make_async_remote_copy(
            src_ref=src, dst_ref=dst, send_sem=send, recv_sem=recv, device_id=device, device_id_type=MESH
        )

    barrier = pltpu.get_barrier_semaphore()

    def hello(shot, tile):
        pl.semaphore_signal(barrier, inc=1, device_id=(shot, tile), device_id_type=MESH)

    for k in range(1, 16):
        hello((s_i + k) % 16, t_i)
    for k in range(1, 8):
        hello(s_i, (t_i + k) % 8)

    @pl.when(elsewhere)
    def _():
        hello((2 * d + half - 2 * t_i + 16) % 16, t_i)

    for k in range(8):
        tile = (t_i + k) % 8
        for c in range(2):
            if k + c:
                hello((2 * d + (half + c) % 2 - 2 * tile + 16) % 16, tile)

    for m, ref in enumerate((lam, mu, buoy)):
        TM[m] = ref[...].T
    for f in range(9):
        T[f] = wave[f].T

    SZ[:, 0:4] = jnp.zeros((3, 4, 8, 128), F32)
    SZ[:, 36:40] = jnp.zeros((3, 4, 8, 128), F32)

    def blank(side):
        for par in range(2):
            HR[par, side] = jnp.zeros((3, 4, 8, 128), F32)
            QR[par, side] = jnp.zeros((3, 4, 8, 128), F32)
        B[36 * side : 36 * side + 4] = jnp.zeros((4, 8, 128), F32)

    pl.when(jnp.logical_not(has_left))(lambda: blank(0))
    pl.when(jnp.logical_not(has_right))(lambda: blank(1))

    pl.semaphore_wait(barrier, 15 + 7 + 15 + elsewhere.astype(jnp.int32))

    def spread_material(k):
        p = (s_i + k) % 16
        rows = 16 * ((p + 2 * t_i) % 16)
        return remote(TM.at[:, pl.ds(rows, 16), :], G.at[s_i], m_send.at[k], m_recv, (p, t_i))

    spread = [spread_material(k) for k in range(1, 16)]
    for copy in spread:
        copy.start()
    pltpu.make_async_copy(TM.at[:, pl.ds(16 * piece, 16), :], G.at[s_i], m_recv).start()

    def move_wave(k):
        to = 4 * ((t_i // 4 + k // 4) % 2) + (t_i + k) % 4
        dd = snake(to)
        return remote(
            T.at[:, pl.ds(32 * dd, 32), :],
            RW.at[:, pl.ds(32 * t_i, 32), :],
            w_send.at[k],
            w_recv,
            (s_i, snake(dd)),
        )

    waves = [move_wave(k) for k in WAVE_ORDER]
    for i in (0, 1, 2, 5, 6):
        waves[i].start()
    pltpu.make_async_copy(T.at[:, pl.ds(32 * d, 32), :], RW.at[:, pl.ds(32 * t_i, 32), :], w_recv).start()

    iota = lax.broadcasted_iota(jnp.int32, (128, 128), 1)
    for part in range(2):
        ids = jnp.broadcast_to(receivers[:, 128 * part : 128 * part + 128], (128, 128)).astype(F32)
        ids = ids.T.astype(jnp.int32)
        z = ids & 255
        y = (ids >> 8) & 31
        x = ids >> 13
        mine = (z >> 5) == d
        row = (z & 31) * 8 + (x >> 2)
        lane = (x & 3) * 32 + y
        rows = pl.ds(128 * part, 128)
        for j in range(2):
            hit = jnp.logical_and(mine, row == iota + 128 * j)
            R1[rows, 128 * j : 128 * j + 128] = jnp.where(hit, 1.0, 0.0).astype(BF16)
        here = jnp.where(lane == iota, 1.0, 0.0)
        L2[rows, 0:128] = here
        L2[rows, 128:256] = here
    IMG[...] = jnp.zeros((32, 8, 128), F32)

    pltpu.make_async_copy(G, G, m_recv).wait()
    for s in range(16):
        M[s] = G[ap_row[s]]

    def send_material(k):
        s = (s_i + k) % 16
        return remote(
            M.at[s],
            RM.at[:, pl.ds(32 * t_i + 16 * half, 16), :],
            n_send.at[k],
            n_recv,
            (s, snake(piece_d)),
        )

    deliver = [send_material(k) for k in range(16)]
    for k in range(1, 16):
        deliver[k].start()

    @pl.when(elsewhere)
    def _():
        deliver[0].start()

    @pl.when(jnp.logical_not(elsewhere))
    def _():
        pltpu.make_async_copy(M.at[s_i], RM.at[:, pl.ds(32 * t_i + 16 * half, 16), :], n_recv).start()

    for i in (3, 4):
        waves[i].start()

    pltpu.make_async_copy(RW, RW, w_recv).wait()
    for z in range(32):
        rows = pl.ds(z, 8, stride=32)
        for j, f in enumerate(WITH_Z):
            SZ[j, 4 + z] = RW[f, rows, :]
        for j, f in enumerate(IN_PLANE):
            SO[j, z] = RW[f, rows, :]
        for j, f in enumerate(VELOCITY):
            V[j, 4 + z] = RW[f, rows, :]

    def halo(par, part):
        def one(side, src, dst, device):
            return remote(src, dst, halo_send.at[par, side, part], halo_recv.at[par, side, part], device)

        if part == 0:
            to_left = one(0, SZ.at[:, 4:8], HR.at[par, 1], left_id)
            to_right = one(1, SZ.at[:, 32:36], HR.at[par, 0], right_id)
        else:
            to_left = one(0, QB.at[par, 0], QR.at[par, 1], left_id)
            to_right = one(1, QB.at[par, 1], QR.at[par, 0], right_id)
        return to_left, to_right

    def start_halo(par, part):
        to_left, to_right = halo(par, part)
        pl.when(has_left)(to_left.start)
        pl.when(has_right)(to_right.start)

    def wait_halo(par):
        for part in range(2):
            to_left, to_right = halo(par, part)

            @pl.when(has_left)
            def _():
                to_left.wait_send()
                to_right.wait_recv()

            @pl.when(has_right)
            def _():
                to_right.wait_send()
                to_left.wait_recv()

    start_halo(0, 0)

    pltpu.make_async_copy(RM, RM, n_recv).wait()
    for z in range(32):
        B[4 + z] = RM[2, pl.ds(z, 8, stride=32), :] * (DT * UNIT)

    b_left = remote(B.at[4:8], B.at[36:40], b_send.at[0], b_recv.at[0], left_id)
    b_right = remote(B.at[32:36], B.at[0:4], b_send.at[1], b_recv.at[1], right_id)
    pl.when(has_left)(b_left.start)
    pl.when(has_right)(b_right.start)

    sub = lax.broadcasted_iota(jnp.int32, (8, 128), 0)
    lane = lax.broadcasted_iota(jnp.int32, (8, 128), 1)
    cell = (4 * sub + lane // 32) * 8192 + (lane % 32) * 256 + 32 * d
    where_source = source[0]
    for z in range(32):
        shear = RM[1, pl.ds(z, 8, stride=32), :] * (DT * UNIT)
        L[z] = RM[0, pl.ds(z, 8, stride=32), :] * (DT * UNIT)
        MU[z] = shear
        MU2[z] = 2.0 * shear
        SRC[z] = jnp.where(cell + z == where_source, RM[2, pl.ds(z, 8, stride=32), :] * DT, 0.0)

    first = (sub == 0)[None]
    last = (sub == 7)[None]

    def flat(value):
        return value.reshape(64, 128)

    def along_x(same, before, after):
        down = jnp.where(first, 0.0, pltpu.roll(before.reshape(8, 8, 128), 1, 1))
        up = jnp.where(last, 0.0, pltpu.roll(after.reshape(8, 8, 128), 7, 1))
        return same.reshape(8, 8, 128) + (down + up)

    def along_z(load):
        total = None
        for k in range(1, 5):
            term = WEIGHTS[k - 1] * (load(k) - load(-k))
            total = term if total is None else total + term
        return total

    def velocity(parts, amplitude):
        def take(ref, *index, shift=0):
            got = [ref[index + (pl.ds(z + shift, n),)] for z, n in parts]
            return got[0] if len(got) == 1 else jnp.concatenate(got, axis=0)

        def with_z(j, shift=0):
            return take(SZ, j, shift=4 + shift)

        fields = (take(SO, 0), take(SO, 2), with_z(0), take(SO, 1), with_z(1))
        xs = jnp.concatenate([split(flat(field)) for field in fields[0:3]], axis=0)
        ys = jnp.concatenate([split(flat(field)) for field in fields[3:5]], axis=0)
        px = jnp.dot(xs, weights[...], preferred_element_type=F32)
        py = jnp.dot(ys, weights[:, 384:512], preferred_element_type=F32)

        def x_of(m):
            rows = px[64 * m : 64 * m + 64]
            return along_x(rows[:, 0:128], rows[:, 128:256], rows[:, 256:384])

        def y_of(rows):
            return rows.reshape(8, 8, 128)

        ys = (y_of(px[64:128, 384:512]), y_of(py[0:64]), y_of(py[64:128]))
        gain = take(B, shift=4)
        new = [
            take(V, j, shift=4) + gain * (x_of(j) + ys[j] + along_z(lambda k: with_z(j, k)))
            for j in range(3)
        ]
        new[2] = new[2] + take(SRC) * amplitude
        return new

    def inner_velocity(z0, amplitude):
        new = velocity([(z0, 8)], amplitude)
        for j in range(3):
            V[j, pl.ds(z0 + 4, 8)] = new[j]

    def partial_velocity(par, amplitude):
        new = velocity([(0, 4), (28, 4)], amplitude)
        for j in range(3):
            QB[par, 0, j] = new[j][0:4]
            QB[par, 1, j] = new[j][4:8]

    def complete_velocity(par):
        for j in range(4):
            low = high = None
            for k in range(j + 1, 5):
                term = WEIGHTS[k - 1] * HR[par, 0, :, 4 + j - k]
                low = term if low is None else low + term
            for k in range(4 - j, 5):
                term = WEIGHTS[k - 1] * HR[par, 1, :, j - 4 + k]
                high = term if high is None else high + term
            V[:, 4 + j] = QB[par, 0, :, j] - B[4 + j] * low
            V[:, 32 + j] = QB[par, 1, :, j] + B[32 + j] * high
            low = high = None
            for k in range(4 - j, 5):
                term = WEIGHTS[k - 1] * SZ[:, j + k]
                low = term if low is None else low + term
            for k in range(j + 1, 5):
                term = WEIGHTS[k - 1] * SZ[:, 36 + j - k]
                high = term if high is None else high + term
            V[:, j] = QR[par, 0, :, j] + B[j] * low
            V[:, 36 + j] = QR[par, 1, :, j] - B[36 + j] * high

    def stresses(z0):
        def speed(j, shift=0):
            return V[j, pl.ds(z0 + 4 + shift, 8)]

        rows = jnp.concatenate([split(flat(speed(j))) for j in range(3)], axis=0)
        p = jnp.dot(rows, weights[...], preferred_element_type=F32)

        def x_of(m):
            r = p[64 * m : 64 * m + 64]
            return along_x(r[:, 0:128], r[:, 128:256], r[:, 256:384])

        def y_of(m):
            return p[64 * m : 64 * m + 64, 384:512].reshape(8, 8, 128)

        at = pl.ds(z0, 8)
        wide = pl.ds(z0 + 4, 8)
        shear = MU[at]
        exx = x_of(0)
        eyy = y_of(1)
        ezz = along_z(lambda k: speed(2, k))
        SZ[0, wide] = SZ[0, wide] + shear * (along_z(lambda k: speed(0, k)) + x_of(2))
        SZ[1, wide] = SZ[1, wide] + shear * (along_z(lambda k: speed(1, k)) + y_of(2))
        SO[2, at] = SO[2, at] + shear * (y_of(0) + x_of(1))
        div = exx + eyy + ezz
        bulk = L[at] * div
        twice = MU2[at]
        szz = SZ[2, wide] + (bulk + twice * ezz)
        sxx = SO[0, at] + (bulk + twice * exx)
        syy = SO[1, at] + (bulk + twice * eyy)
        SZ[2, wide] = szz
        SO[0, at] = sxx
        SO[1, at] = syy
        IMG[at] = IMG[at] + div * (sxx + syy + szz)

    def spread_grad(k):
        p = (s_i + k) % 16
        return remote(grad.at[pl.ds(8 * p, 8), :], GG.at[s_i], g_send.at[k], g_recv, (p, t_i))

    grads = [spread_grad(k) for k in range(1, 16)]
    def start_gradients():
        for copy in grads:
            copy.start()
        pltpu.make_async_copy(grad.at[pl.ds(8 * s_i, 8), :], GG.at[s_i], g_recv).start()

    def send_owner(k):
        q = (s_i + k) % 16
        return remote(MO.at[q], o_owner.at[pl.ds(8 * s_i, 8), :], h_send.at[k], h_recv, (q, t_i))

    owners = [send_owner(k) for k in range(1, 16)]

    def gradients():
        pltpu.make_async_copy(GG, GG, g_recv).wait()
        for q in range(16):
            total = jnp.zeros((8, 256), F32)
            for s in range(16):
                total = total + jnp.where(pr_row[s] == q, GG[s], 0.0)
            MO[q] = total
        for copy in owners:
            copy.start()
        pltpu.make_async_copy(MO.at[s_i], o_owner.at[pl.ds(8 * s_i, 8), :], h_recv).start()

    partial_velocity(0, wavelet[0, 0])
    start_halo(0, 1)

    @pl.when(has_left)
    def _():
        b_left.wait_send()
        b_right.wait_recv()

    @pl.when(has_right)
    def _():
        b_right.wait_send()
        b_left.wait_recv()

    def step(n, carry):
        par = lax.rem(n, 2)
        amplitude = wavelet[0, n]
        for z0 in (4, 12, 20):
            inner_velocity(z0, amplitude)
        wait_halo(par)
        complete_velocity(par)
        for z0 in (0, 24):
            stresses(z0)

        @pl.when(n < STEPS - 1)
        def _():
            start_halo(1 - par, 0)
            partial_velocity(1 - par, wavelet[0, jnp.minimum(n + 1, STEPS - 1)])
            start_halo(1 - par, 1)

        for z0 in (8, 16):
            stresses(z0)
        picked = jnp.dot(R1[...], split(V[2, 4:36].reshape(256, 128)), preferred_element_type=F32)
        picked = (picked * L2[...]).astype(BF16)
        TRB[n] = lax.dot_general(
            jnp.ones((8, 256), BF16), picked, (((1,), (1,)), ((), ())), preferred_element_type=F32
        )
        pl.when(n == 1)(start_gradients)
        pl.when(n == 5)(gradients)
        return carry

    lax.fori_loop(0, STEPS, step, 0)

    for z in range(32):
        rows = pl.ds(z, 8, stride=32)
        for j, f in enumerate(VELOCITY):
            OB[f, rows, :] = V[j, 4 + z]
        for j, f in enumerate(WITH_Z):
            OB[f, rows, :] = SZ[j, 4 + z]
        for j, f in enumerate(IN_PLANE):
            OB[f, rows, :] = SO[j, z]
        OB[9, rows, :] = IMG[z] * UNIT

    def send_home(k):
        t = 4 * ((t_i // 4 + k // 4) % 2) + (t_i + k) % 4
        return remote(
            OB.at[:, pl.ds(32 * t, 32), :],
            o_planes.at[:, pl.ds(32 * d, 32), :],
            o_send.at[k],
            o_recv,
            (s_i, t),
        )

    homes = [send_home(k) for k in WAVE_ORDER]
    for copy in homes:
        copy.start()
    pltpu.make_async_copy(
        OB.at[:, pl.ds(32 * t_i, 32), :], o_planes.at[:, pl.ds(32 * d, 32), :], o_recv
    ).start()

    for n in range(STEPS):
        TRS[n : n + 1, :] = TRB[n, 0:1, :]

    def send_trace(k):
        return remote(TRS, TRR.at[d], t_send.at[k], t_recv, (s_i, snake((d + k) % 8)))

    traces = [send_trace(k) for k in range(1, 8)]
    for copy in traces:
        copy.start()
    pltpu.make_async_copy(TRS, TRR.at[d], t_recv).start()

    for copies in (spread, grads, owners, waves):
        for copy in copies:
            copy.wait_send()
    for k in range(1, 16):
        deliver[k].wait_send()
    pl.when(elsewhere)(deliver[0].wait_send)
    pltpu.make_async_copy(o_owner, o_owner, h_recv).wait()

    pltpu.make_async_copy(TRR, TRR, t_recv).wait()
    total = TRR[0]
    for j in range(1, 8):
        total = total + TRR[j]
    o_trace[...] = total

    pltpu.make_async_copy(o_planes, o_planes, o_recv).wait()
    for copy in homes + traces:
        copy.wait_send()


def finish(planes, owner, trace, o_state, o_image, o_owner, o_trace):
    for f in range(9):
        o_state[f] = planes[f].T
    o_image[...] = planes[9].T
    o_owner[...] = owner[...]
    for n in range(STEPS):
        o_trace[n] = trace[n : n + 1, :]


def on_device(
    lame_lambda, lame_mu, buoyancy, aperture_row, wave_state, source_cell, wavelet, receiver_cell,
    prev_row, prev_grad,
):
    weights = jnp.asarray(operators(), BF16)
    vmem = pl.BlockSpec(memory_space=pltpu.VMEM)
    smem = pl.BlockSpec(memory_space=pltpu.SMEM)
    dma = pltpu.SemaphoreType.DMA
    tile = (8, 128)
    planes, owner, trace = pl.pallas_call(
        kernel,
        out_shape=(
            jax.ShapeDtypeStruct((10, 256, 128), F32),
            jax.ShapeDtypeStruct((128, 256), F32),
            jax.ShapeDtypeStruct((STEPS, 256), F32),
        ),
        in_specs=[smem] * 4 + [vmem] * 7,
        out_specs=(pl.BlockSpec(memory_space=pl.ANY), vmem, vmem),
        scratch_shapes=[
            pltpu.VMEM((9, 256, 128), F32),
            pltpu.VMEM((9, 256, 128), F32),
            pltpu.VMEM((3, 256, 128), F32),
            pltpu.VMEM((16, 3, 16, 128), F32),
            pltpu.VMEM((16, 3, 16, 128), F32),
            pltpu.VMEM((3, 256, 128), F32),
            pltpu.VMEM((16, 8, 256), F32),
            pltpu.VMEM((16, 8, 256), F32),
            pltpu.VMEM((3, 40) + tile, F32),
            pltpu.VMEM((3, 32) + tile, F32),
            pltpu.VMEM((3, 40) + tile, F32),
            pltpu.VMEM((40,) + tile, F32),
            pltpu.VMEM((32,) + tile, F32),
            pltpu.VMEM((32,) + tile, F32),
            pltpu.VMEM((32,) + tile, F32),
            pltpu.VMEM((32,) + tile, F32),
            pltpu.VMEM((32,) + tile, F32),
            pltpu.VMEM((2, 2, 3, 4) + tile, F32),
            pltpu.VMEM((2, 2, 3, 4) + tile, F32),
            pltpu.VMEM((2, 2, 3, 4) + tile, F32),
            pltpu.VMEM((256, 256), BF16),
            pltpu.VMEM((256, 256), F32),
            pltpu.VMEM((STEPS, 8, 256), F32),
            pltpu.VMEM((STEPS, 256), F32),
            pltpu.VMEM((8, STEPS, 256), F32),
            pltpu.VMEM((10, 256, 128), F32),
            dma((8,)), dma, dma((16,)), dma, dma((16,)), dma, dma((16,)), dma, dma((16,)), dma,
            dma((2, 2, 2)), dma((2, 2, 2)), dma((2,)), dma((2,)), dma((8,)), dma, dma((8,)), dma,
        ],
        compiler_params=pltpu.CompilerParams(collective_id=0, has_side_effects=True),
        name="wave",
    )(
        aperture_row,
        prev_row,
        source_cell,
        wavelet,
        receiver_cell,
        wave_state.reshape(9, 128, 256),
        lame_lambda.reshape(128, 256),
        lame_mu.reshape(128, 256),
        buoyancy.reshape(128, 256),
        prev_grad.reshape(128, 256),
        weights,
    )
    state, image, owner, trace = pl.pallas_call(
        finish,
        out_shape=(
            jax.ShapeDtypeStruct((9, 128, 256), F32),
            jax.ShapeDtypeStruct((128, 256), F32),
            jax.ShapeDtypeStruct((128, 256), F32),
            jax.ShapeDtypeStruct((STEPS, 1, 256), F32),
        ),
        in_specs=[vmem] * 3,
        out_specs=(vmem,) * 4,
        name="finish",
    )(planes, owner, trace)
    return (
        state.reshape(1, 9, 4, 32, 256),
        image.reshape(1, 4, 32, 256),
        owner.reshape(4, 32, 256),
        jnp.transpose(trace, (1, 0, 2)),
    )


def solution(mesh):
    placed = (
        P(("shot", "tile"), None, None),
        P(("shot", "tile"), None, None),
        P(("shot", "tile"), None, None),
        P(),
        P("shot", None, "tile", None, None),
        P("shot"),
        P("shot", None),
        P("shot", None),
        P(),
        P("shot", "tile", None, None),
    )
    return jax.shard_map(
        on_device,
        mesh=mesh,
        in_specs=placed,
        out_specs=(
            P("shot", None, "tile", None, None),
            P("shot", "tile", None, None),
            P(("shot", "tile"), None, None),
            P("shot", None, None),
        ),
        check_vma=False,
    )
```

```python
import jax
import jax.numpy as jnp
import numpy as np
from jax import lax
from jax.experimental import pallas as pl
from jax.experimental.pallas import tpu as pltpu
from jax.sharding import PartitionSpec as P

MESH = pl.DeviceIdType.MESH
F32 = jnp.float32
BF16 = jnp.bfloat16

WEIGHTS = (672.0, -168.0, 32.0, -3.0)
UNIT = 1.0 / 840.0
DT = 0.2
STEPS = 12

WAVE_ORDER = (1, 3, 2, 4, 5, 7, 6)

VELOCITY = (0, 1, 2)
WITH_Z = (7, 8, 5)
IN_PLANE = (3, 4, 6)


def operators():
    gain = np.zeros(9)
    for k in range(1, 5):
        gain[4 + k] = WEIGHTS[k - 1]
        gain[4 - k] = -WEIGHTS[k - 1]

    def at(diff):
        return np.where(np.abs(diff) <= 4, gain[np.clip(diff, -4, 4) + 4], 0.0)

    lane = np.arange(128)
    x, y = lane // 32, lane % 32
    dx = x[:, None] - x[None, :]
    dy = y[:, None] - y[None, :]
    same_y = (dy == 0).astype(np.float64)
    same_x = (dx == 0).astype(np.float64)
    block = np.concatenate(
        [at(dx) * same_y, at(dx - 4) * same_y, at(dx + 4) * same_y, at(dy) * same_x], axis=1
    )
    return np.concatenate([block, block], axis=0)


def split(rows):
    hi = rows.astype(BF16)
    lo = (rows - hi.astype(F32)).astype(BF16)
    return jnp.concatenate([hi, lo], axis=1)


def kernel(
    ap_row, pr_row, source, wavelet, receivers, wave_in, lam_in, mu_in, buoy_in, grad_in, weights_in,
    o_planes, o_owner, o_trace,
    wave, mats, grad, weights, T, RW, TM, G, M, RM, GG, MO,
    PRM, PRO, PR, SZ, SO, V, B, L, MU, MU2, SRC, IMG, HR, QB, QR, R1, L2, TRB, TRS, TRR, OB,
    i_sem, w_send, w_recv, m_send, m_recv, n_send, n_recv, g_send, g_recv, h_send, h_recv,
    p_send, p_recv, halo_send, halo_recv, b_send, b_recv, t_send, t_recv, o_send, o_recv,
):
    s_i = lax.axis_index("shot")
    t_i = lax.axis_index("tile")

    def snake(i):
        return jnp.where(i < 4, i, 11 - i)

    d = snake(t_i)
    core = s_i % 2
    base = s_i - core
    swapped = d % 2 == 1
    role = base + (core + d) % 2
    piece = (s_i + 2 * t_i) % 16
    piece_d = piece // 2
    half = piece % 2
    elsewhere = piece_d != d
    has_left = d > 0
    has_right = d < 7
    left_id = (base + 1 - core, snake(jnp.maximum(d - 1, 0)))
    right_id = (base + 1 - core, snake(jnp.minimum(d + 1, 7)))

    def remote(src, dst, send, recv, device):
        return pltpu.make_async_remote_copy(
            src_ref=src, dst_ref=dst, send_sem=send, recv_sem=recv, device_id=device, device_id_type=MESH
        )

    loads = [
        pltpu.make_async_copy(src, dst, i_sem.at[i])
        for i, (src, dst) in enumerate(
            (
                (lam_in, mats.at[0]),
                (mu_in, mats.at[1]),
                (buoy_in, mats.at[2]),
                (wave_in, wave),
                (grad_in, grad),
                (weights_in, weights),
            )
        )
    ]
    for load in loads:
        load.start()

    barrier = pltpu.get_barrier_semaphore()

    def hello(shot, tile):
        pl.semaphore_signal(barrier, inc=1, device_id=(shot, tile), device_id_type=MESH)

    for k in range(1, 16):
        hello((s_i + k) % 16, t_i)
    for k in range(1, 8):
        for c in range(2):
            hello(base + c, (t_i + k) % 8)

    @pl.when(elsewhere)
    def _():
        hello((2 * d + half - 2 * t_i + 16) % 16, t_i)

    for k in range(8):
        tile = (t_i + k) % 8
        for c in range(2):
            if k + c:
                hello((2 * d + (half + c) % 2 - 2 * tile + 16) % 16, tile)

    for m in range(3):
        loads[m].wait()
        TM[m] = mats[m].T
    loads[3].wait()
    for f in range(9):
        T[f] = wave[f].T
    loads[4].wait()
    loads[5].wait()

    for n in range(STEPS):
        PRM[n : n + 1, :] = jnp.full((1, 128), wavelet[0, n], F32)
    for part in range(2):
        PRM[16 + part : 17 + part, :] = receivers[:, 128 * part : 128 * part + 128].astype(F32)
    PRM[18:19, :] = jnp.full((1, 128), source[0], jnp.int32).astype(F32)

    SZ[:, 0:4] = jnp.zeros((3, 4, 8, 128), F32)
    SZ[:, 36:40] = jnp.zeros((3, 4, 8, 128), F32)

    def blank(side):
        for par in range(2):
            HR[par, side] = jnp.zeros((3, 4, 8, 128), F32)
            QR[par, side] = jnp.zeros((3, 4, 8, 128), F32)
        B[36 * side : 36 * side + 4] = jnp.zeros((4, 8, 128), F32)

    pl.when(jnp.logical_not(has_left))(lambda: blank(0))
    pl.when(jnp.logical_not(has_right))(lambda: blank(1))

    pl.semaphore_wait(barrier, 15 + 14 + 15 + elsewhere.astype(jnp.int32))

    def spread_material(k):
        p = (s_i + k) % 16
        rows = 16 * ((p + 2 * t_i) % 16)
        return remote(TM.at[:, pl.ds(rows, 16), :], G.at[s_i], m_send.at[k], m_recv, (p, t_i))

    spread = [spread_material(k) for k in range(1, 16)]
    for copy in spread:
        copy.start()
    pltpu.make_async_copy(TM.at[:, pl.ds(16 * piece, 16), :], G.at[s_i], m_recv).start()

    table = remote(PRM, PRO, p_send, p_recv, (base + 1 - core, t_i))
    table.start()

    def move_wave(k):
        to = 4 * ((t_i // 4 + k // 4) % 2) + (t_i + k) % 4
        dd = snake(to)
        return remote(
            T.at[:, pl.ds(32 * dd, 32), :],
            RW.at[:, pl.ds(32 * t_i, 32), :],
            w_send.at[k],
            w_recv,
            (base + (core + dd) % 2, to),
        )

    waves = [move_wave(k) for k in WAVE_ORDER]
    wave_near = move_wave(0)

    @pl.when(core == 0)
    def _():
        for i in (3, 0, 4, 1, 5, 2, 6):
            waves[i].start()

    @pl.when(core == 1)
    def _():
        for i in (0, 1, 2):
            waves[i].start()


    pl.when(swapped)(wave_near.start)

    @pl.when(jnp.logical_not(swapped))
    def _():
        pltpu.make_async_copy(
            T.at[:, pl.ds(32 * d, 32), :], RW.at[:, pl.ds(32 * t_i, 32), :], w_recv
        ).start()

    table.wait()

    @pl.when(swapped)
    def _():
        PR[...] = PRO[...]

    @pl.when(jnp.logical_not(swapped))
    def _():
        PR[...] = PRM[...]

    iota = lax.broadcasted_iota(jnp.int32, (128, 128), 1)
    for part in range(2):
        ids = jnp.broadcast_to(PR[16 + part : 17 + part, :], (128, 128)).T.astype(jnp.int32)
        z = ids & 255
        y = (ids >> 8) & 31
        x = ids >> 13
        mine = (z >> 5) == d
        row = (z & 31) * 8 + (x >> 2)
        lane = (x & 3) * 32 + y
        rows = pl.ds(128 * part, 128)
        for j in range(2):
            hit = jnp.logical_and(mine, row == iota + 128 * j)
            R1[rows, 128 * j : 128 * j + 128] = jnp.where(hit, 1.0, 0.0).astype(BF16)
        here = jnp.where(lane == iota, 1.0, 0.0)
        L2[rows, 0:128] = here
        L2[rows, 128:256] = here
    IMG[...] = jnp.zeros((32, 8, 128), F32)

    pltpu.make_async_copy(G, G, m_recv).wait()
    for s in range(16):
        M[s] = G[ap_row[s]]

    def send_material(k):
        s = (role + k) % 16
        return remote(
            M.at[s],
            RM.at[:, pl.ds(32 * t_i + 16 * half, 16), :],
            n_send.at[k],
            n_recv,
            (s - s % 2 + (s % 2 + piece_d) % 2, snake(piece_d)),
        )

    deliver = [send_material(k) for k in range(16)]
    for k in range(1, 16):
        deliver[k].start()

    @pl.when(elsewhere)
    def _():
        deliver[0].start()

    @pl.when(jnp.logical_not(elsewhere))
    def _():
        pltpu.make_async_copy(M.at[role], RM.at[:, pl.ds(32 * t_i + 16 * half, 16), :], n_recv).start()


    @pl.when(core == 1)
    def _():
        for i in (3, 4, 5, 6):
            waves[i].start()

    pltpu.make_async_copy(RW, RW, w_recv).wait()
    for z in range(32):
        rows = pl.ds(z, 8, stride=32)
        for j, f in enumerate(WITH_Z):
            SZ[j, 4 + z] = RW[f, rows, :]
        for j, f in enumerate(IN_PLANE):
            SO[j, z] = RW[f, rows, :]
        for j, f in enumerate(VELOCITY):
            V[j, 4 + z] = RW[f, rows, :]

    def halo(par, part):
        def one(side, src, dst, device):
            return remote(src, dst, halo_send.at[par, side, part], halo_recv.at[par, side, part], device)

        if part == 0:
            to_left = one(0, SZ.at[:, 4:8], HR.at[par, 1], left_id)
            to_right = one(1, SZ.at[:, 32:36], HR.at[par, 0], right_id)
        else:
            to_left = one(0, QB.at[par, 0], QR.at[par, 1], left_id)
            to_right = one(1, QB.at[par, 1], QR.at[par, 0], right_id)
        return to_left, to_right

    def start_halo(par, part):
        to_left, to_right = halo(par, part)
        pl.when(has_left)(to_left.start)
        pl.when(has_right)(to_right.start)

    def wait_halo(par):
        for part in range(2):
            to_left, to_right = halo(par, part)

            @pl.when(has_left)
            def _():
                to_left.wait_send()
                to_right.wait_recv()

            @pl.when(has_right)
            def _():
                to_right.wait_send()
                to_left.wait_recv()

    start_halo(0, 0)

    pltpu.make_async_copy(RM, RM, n_recv).wait()
    for z in range(32):
        B[4 + z] = RM[2, pl.ds(z, 8, stride=32), :] * (DT * UNIT)

    b_left = remote(B.at[4:8], B.at[36:40], b_send.at[0], b_recv.at[0], left_id)
    b_right = remote(B.at[32:36], B.at[0:4], b_send.at[1], b_recv.at[1], right_id)
    pl.when(has_left)(b_left.start)
    pl.when(has_right)(b_right.start)

    sub = lax.broadcasted_iota(jnp.int32, (8, 128), 0)
    lane = lax.broadcasted_iota(jnp.int32, (8, 128), 1)
    cell = (4 * sub + lane // 32) * 8192 + (lane % 32) * 256 + 32 * d
    where_source = PR[18:19, :].astype(jnp.int32)
    for z in range(32):
        shear = RM[1, pl.ds(z, 8, stride=32), :] * (DT * UNIT)
        L[z] = RM[0, pl.ds(z, 8, stride=32), :] * (DT * UNIT)
        MU[z] = shear
        MU2[z] = 2.0 * shear
        SRC[z] = jnp.where(cell + z == where_source, RM[2, pl.ds(z, 8, stride=32), :] * DT, 0.0)

    first = (sub == 0)[None]
    last = (sub == 7)[None]

    def flat(value):
        return value.reshape(64, 128)

    def along_x(same, before, after):
        down = jnp.where(first, 0.0, pltpu.roll(before.reshape(8, 8, 128), 1, 1))
        up = jnp.where(last, 0.0, pltpu.roll(after.reshape(8, 8, 128), 7, 1))
        return same.reshape(8, 8, 128) + (down + up)

    def along_z(load):
        total = None
        for k in range(1, 5):
            term = WEIGHTS[k - 1] * (load(k) - load(-k))
            total = term if total is None else total + term
        return total

    def velocity(parts, amplitude):
        def take(ref, *index, shift=0):
            got = [ref[index + (pl.ds(z + shift, n),)] for z, n in parts]
            return got[0] if len(got) == 1 else jnp.concatenate(got, axis=0)

        def with_z(j, shift=0):
            return take(SZ, j, shift=4 + shift)

        fields = (take(SO, 0), take(SO, 2), with_z(0), take(SO, 1), with_z(1))
        xs = jnp.concatenate([split(flat(field)) for field in fields[0:3]], axis=0)
        ys = jnp.concatenate([split(flat(field)) for field in fields[3:5]], axis=0)
        px = jnp.dot(xs, weights[...], preferred_element_type=F32)
        py = jnp.dot(ys, weights[:, 384:512], preferred_element_type=F32)

        def x_of(m):
            rows = px[64 * m : 64 * m + 64]
            return along_x(rows[:, 0:128], rows[:, 128:256], rows[:, 256:384])

        def y_of(rows):
            return rows.reshape(8, 8, 128)

        ys = (y_of(px[64:128, 384:512]), y_of(py[0:64]), y_of(py[64:128]))
        gain = take(B, shift=4)
        new = [
            take(V, j, shift=4) + gain * (x_of(j) + ys[j] + along_z(lambda k: with_z(j, k)))
            for j in range(3)
        ]
        new[2] = new[2] + take(SRC) * amplitude
        return new

    def inner_velocity(z0, amplitude):
        new = velocity([(z0, 8)], amplitude)
        for j in range(3):
            V[j, pl.ds(z0 + 4, 8)] = new[j]

    def partial_velocity(par, amplitude):
        new = velocity([(0, 4), (28, 4)], amplitude)
        for j in range(3):
            QB[par, 0, j] = new[j][0:4]
            QB[par, 1, j] = new[j][4:8]

    def complete_velocity(par):
        for j in range(4):
            low = high = None
            for k in range(j + 1, 5):
                term = WEIGHTS[k - 1] * HR[par, 0, :, 4 + j - k]
                low = term if low is None else low + term
            for k in range(4 - j, 5):
                term = WEIGHTS[k - 1] * HR[par, 1, :, j - 4 + k]
                high = term if high is None else high + term
            V[:, 4 + j] = QB[par, 0, :, j] - B[4 + j] * low
            V[:, 32 + j] = QB[par, 1, :, j] + B[32 + j] * high
            low = high = None
            for k in range(4 - j, 5):
                term = WEIGHTS[k - 1] * SZ[:, j + k]
                low = term if low is None else low + term
            for k in range(j + 1, 5):
                term = WEIGHTS[k - 1] * SZ[:, 36 + j - k]
                high = term if high is None else high + term
            V[:, j] = QR[par, 0, :, j] + B[j] * low
            V[:, 36 + j] = QR[par, 1, :, j] - B[36 + j] * high

    def stresses(z0):
        def speed(j, shift=0):
            return V[j, pl.ds(z0 + 4 + shift, 8)]

        rows = jnp.concatenate([split(flat(speed(j))) for j in range(3)], axis=0)
        p = jnp.dot(rows, weights[...], preferred_element_type=F32)

        def x_of(m):
            r = p[64 * m : 64 * m + 64]
            return along_x(r[:, 0:128], r[:, 128:256], r[:, 256:384])

        def y_of(m):
            return p[64 * m : 64 * m + 64, 384:512].reshape(8, 8, 128)

        at = pl.ds(z0, 8)
        wide = pl.ds(z0 + 4, 8)
        shear = MU[at]
        exx = x_of(0)
        eyy = y_of(1)
        ezz = along_z(lambda k: speed(2, k))
        SZ[0, wide] = SZ[0, wide] + shear * (along_z(lambda k: speed(0, k)) + x_of(2))
        SZ[1, wide] = SZ[1, wide] + shear * (along_z(lambda k: speed(1, k)) + y_of(2))
        SO[2, at] = SO[2, at] + shear * (y_of(0) + x_of(1))
        div = exx + eyy + ezz
        bulk = L[at] * div
        twice = MU2[at]
        szz = SZ[2, wide] + (bulk + twice * ezz)
        sxx = SO[0, at] + (bulk + twice * exx)
        syy = SO[1, at] + (bulk + twice * eyy)
        SZ[2, wide] = szz
        SO[0, at] = sxx
        SO[1, at] = syy
        IMG[at] = IMG[at] + div * (sxx + syy + szz)

    def spread_grad(k):
        p = (s_i + k) % 16
        return remote(grad.at[pl.ds(8 * p, 8), :], GG.at[s_i], g_send.at[k], g_recv, (p, t_i))

    grads = [spread_grad(k) for k in range(1, 16)]
    def start_gradients():
        for copy in grads:
            copy.start()
        pltpu.make_async_copy(grad.at[pl.ds(8 * s_i, 8), :], GG.at[s_i], g_recv).start()

    def send_owner(k):
        q = (s_i + k) % 16
        return remote(MO.at[q], o_owner.at[pl.ds(8 * s_i, 8), :], h_send.at[k], h_recv, (q, t_i))

    owners = [send_owner(k) for k in range(1, 16)]

    def gradients():
        pltpu.make_async_copy(GG, GG, g_recv).wait()
        for q in range(16):
            total = jnp.zeros((8, 256), F32)
            for s in range(16):
                total = total + jnp.where(pr_row[s] == q, GG[s], 0.0)
            MO[q] = total
        for copy in owners:
            copy.start()
        pltpu.make_async_copy(MO.at[s_i], o_owner.at[pl.ds(8 * s_i, 8), :], h_recv).start()

    partial_velocity(0, PR[0:1, :])
    start_halo(0, 1)

    @pl.when(has_left)
    def _():
        b_left.wait_send()
        b_right.wait_recv()

    @pl.when(has_right)
    def _():
        b_right.wait_send()
        b_left.wait_recv()

    def send_home(part, k):
        t = 4 * ((t_i // 4 + k // 4) % 2) + (t_i + k) % 4
        fields = pl.ds(0, 3) if part == 0 else pl.ds(3, 7)
        return remote(
            OB.at[fields, pl.ds(32 * t, 32), :],
            o_planes.at[fields, pl.ds(32 * d, 32), :],
            o_send.at[part, k],
            o_recv,
            (role, t),
        )

    homes = [[send_home(part, k) for k in (0,) + WAVE_ORDER] for part in range(2)]

    def start_home(part):
        for copy in homes[part][1:]:
            copy.start()
        pl.when(swapped)(homes[part][0].start)
        fields = pl.ds(0, 3) if part == 0 else pl.ds(3, 7)

        @pl.when(jnp.logical_not(swapped))
        def _():
            pltpu.make_async_copy(
                OB.at[fields, pl.ds(32 * t_i, 32), :], o_planes.at[fields, pl.ds(32 * d, 32), :], o_recv
            ).start()

    def velocities_home():
        for z in range(32):
            rows = pl.ds(z, 8, stride=32)
            for j, f in enumerate(VELOCITY):
                OB[f, rows, :] = V[j, 4 + z]
        start_home(0)

    def step(n, carry):
        par = lax.rem(n, 2)
        amplitude = PR[pl.ds(n, 1), :]
        for z0 in (4, 12, 20):
            inner_velocity(z0, amplitude)
        wait_halo(par)
        complete_velocity(par)
        pl.when(n == STEPS - 1)(velocities_home)
        for z0 in (0, 24):
            stresses(z0)

        @pl.when(n < STEPS - 1)
        def _():
            start_halo(1 - par, 0)
            partial_velocity(1 - par, PR[pl.ds(n + 1, 1), :])
            start_halo(1 - par, 1)

        for z0 in (8, 16):
            stresses(z0)
        picked = jnp.dot(R1[...], split(V[2, 4:36].reshape(256, 128)), preferred_element_type=F32)
        picked = (picked * L2[...]).astype(BF16)
        TRB[n] = lax.dot_general(
            jnp.ones((8, 256), BF16), picked, (((1,), (1,)), ((), ())), preferred_element_type=F32
        )
        pl.when(n == 1)(start_gradients)
        pl.when(n == 5)(gradients)
        return carry

    lax.fori_loop(0, STEPS, step, 0)

    for z in range(32):
        rows = pl.ds(z, 8, stride=32)
        for j, f in enumerate(WITH_Z):
            OB[f, rows, :] = SZ[j, 4 + z]
        for j, f in enumerate(IN_PLANE):
            OB[f, rows, :] = SO[j, z]
        OB[9, rows, :] = IMG[z] * UNIT
    start_home(1)

    for n in range(STEPS):
        TRS[n : n + 1, :] = TRB[n, 0:1, :]

    def send_trace(k):
        return remote(TRS, TRR.at[d], t_send.at[k], t_recv, (role, (t_i + k) % 8))

    traces = [send_trace(k) for k in range(8)]
    for copy in traces[1:]:
        copy.start()
    pl.when(swapped)(traces[0].start)

    @pl.when(jnp.logical_not(swapped))
    def _():
        pltpu.make_async_copy(TRS, TRR.at[d], t_recv).start()

    for copies in (spread, grads, owners, waves):
        for copy in copies:
            copy.wait_send()
    pl.when(swapped)(wave_near.wait_send)
    for k in range(1, 16):
        deliver[k].wait_send()
    pl.when(elsewhere)(deliver[0].wait_send)
    pltpu.make_async_copy(o_owner, o_owner, h_recv).wait()

    pltpu.make_async_copy(TRR, TRR, t_recv).wait()
    total = TRR[0]
    for j in range(1, 8):
        total = total + TRR[j]
    o_trace[...] = total

    pltpu.make_async_copy(o_planes, o_planes, o_recv).wait()
    for copy in homes[0][1:] + homes[1][1:] + traces[1:]:
        copy.wait_send()

    @pl.when(swapped)
    def _():
        for copy in (homes[0][0], homes[1][0], traces[0]):
            copy.wait_send()


def finish(planes, owner, trace, o_state, o_image, o_owner, o_trace):
    for f in range(9):
        o_state[f] = planes[f].T
    o_image[...] = planes[9].T
    o_owner[...] = owner[...]
    for n in range(STEPS):
        o_trace[n] = trace[n : n + 1, :]


def on_device(
    lame_lambda, lame_mu, buoyancy, aperture_row, wave_state, source_cell, wavelet, receiver_cell,
    prev_row, prev_grad,
):
    weights = jnp.asarray(operators(), BF16)
    vmem = pl.BlockSpec(memory_space=pltpu.VMEM)
    smem = pl.BlockSpec(memory_space=pltpu.SMEM)
    dma = pltpu.SemaphoreType.DMA
    tile = (8, 128)
    planes, owner, trace = pl.pallas_call(
        kernel,
        out_shape=(
            jax.ShapeDtypeStruct((10, 256, 128), F32),
            jax.ShapeDtypeStruct((128, 256), F32),
            jax.ShapeDtypeStruct((STEPS, 256), F32),
        ),
        in_specs=[smem] * 4 + [vmem] + [pl.BlockSpec(memory_space=pl.ANY)] * 6,
        out_specs=(pl.BlockSpec(memory_space=pl.ANY), vmem, vmem),
        scratch_shapes=[
            pltpu.VMEM((9, 128, 256), F32),
            pltpu.VMEM((3, 128, 256), F32),
            pltpu.VMEM((128, 256), F32),
            pltpu.VMEM((256, 512), BF16),
            pltpu.VMEM((9, 256, 128), F32),
            pltpu.VMEM((9, 256, 128), F32),
            pltpu.VMEM((3, 256, 128), F32),
            pltpu.VMEM((16, 3, 16, 128), F32),
            pltpu.VMEM((16, 3, 16, 128), F32),
            pltpu.VMEM((3, 256, 128), F32),
            pltpu.VMEM((16, 8, 256), F32),
            pltpu.VMEM((16, 8, 256), F32),
            pltpu.VMEM((24, 128), F32),
            pltpu.VMEM((24, 128), F32),
            pltpu.VMEM((24, 128), F32),
            pltpu.VMEM((3, 40) + tile, F32),
            pltpu.VMEM((3, 32) + tile, F32),
            pltpu.VMEM((3, 40) + tile, F32),
            pltpu.VMEM((40,) + tile, F32),
            pltpu.VMEM((32,) + tile, F32),
            pltpu.VMEM((32,) + tile, F32),
            pltpu.VMEM((32,) + tile, F32),
            pltpu.VMEM((32,) + tile, F32),
            pltpu.VMEM((32,) + tile, F32),
            pltpu.VMEM((2, 2, 3, 4) + tile, F32),
            pltpu.VMEM((2, 2, 3, 4) + tile, F32),
            pltpu.VMEM((2, 2, 3, 4) + tile, F32),
            pltpu.VMEM((256, 256), BF16),
            pltpu.VMEM((256, 256), F32),
            pltpu.VMEM((STEPS, 8, 256), F32),
            pltpu.VMEM((STEPS, 256), F32),
            pltpu.VMEM((8, STEPS, 256), F32),
            pltpu.VMEM((10, 256, 128), F32),
            dma((6,)), dma((8,)), dma, dma((16,)), dma, dma((16,)), dma, dma((16,)), dma, dma((16,)), dma,
            dma, dma, dma((2, 2, 2)), dma((2, 2, 2)), dma((2,)), dma((2,)), dma((8,)), dma, dma((2, 8)), dma,
        ],
        compiler_params=pltpu.CompilerParams(collective_id=0, has_side_effects=True),
        name="wave",
    )(
        aperture_row,
        prev_row,
        source_cell,
        wavelet,
        receiver_cell,
        wave_state.reshape(9, 128, 256),
        lame_lambda.reshape(128, 256),
        lame_mu.reshape(128, 256),
        buoyancy.reshape(128, 256),
        prev_grad.reshape(128, 256),
        weights,
    )
    state, image, owner, trace = pl.pallas_call(
        finish,
        out_shape=(
            jax.ShapeDtypeStruct((9, 128, 256), F32),
            jax.ShapeDtypeStruct((128, 256), F32),
            jax.ShapeDtypeStruct((128, 256), F32),
            jax.ShapeDtypeStruct((STEPS, 1, 256), F32),
        ),
        in_specs=[vmem] * 3,
        out_specs=(vmem,) * 4,
        name="finish",
    )(planes, owner, trace)
    return (
        state.reshape(1, 9, 4, 32, 256),
        image.reshape(1, 4, 32, 256),
        owner.reshape(4, 32, 256),
        jnp.transpose(trace, (1, 0, 2)),
    )


def solution(mesh):
    placed = (
        P(("shot", "tile"), None, None),
        P(("shot", "tile"), None, None),
        P(("shot", "tile"), None, None),
        P(),
        P("shot", None, "tile", None, None),
        P("shot"),
        P("shot", None),
        P("shot", None),
        P(),
        P("shot", "tile", None, None),
    )
    return jax.shard_map(
        on_device,
        mesh=mesh,
        in_specs=placed,
        out_specs=(
            P("shot", None, "tile", None, None),
            P("shot", "tile", None, None),
            P(("shot", "tile"), None, None),
            P("shot", None, None),
        ),
        check_vma=False,
    )
```

```python
import jax
import jax.numpy as jnp
import numpy as np
from jax import lax
from jax.experimental import pallas as pl
from jax.experimental.pallas import tpu as pltpu
from jax.sharding import PartitionSpec as P

MESH = pl.DeviceIdType.MESH
F32 = jnp.float32
BF16 = jnp.bfloat16

WEIGHTS = (672.0, -168.0, 32.0, -3.0)
UNIT = 1.0 / 840.0
DT = 0.2
STEPS = 12

WAVE_ORDER = (1, 3, 2, 4, 5, 7, 6)

VELOCITY = (0, 1, 2)
WITH_Z = (7, 8, 5)
IN_PLANE = (3, 4, 6)


def operators():
    gain = np.zeros(9)
    for k in range(1, 5):
        gain[4 + k] = WEIGHTS[k - 1]
        gain[4 - k] = -WEIGHTS[k - 1]

    def at(diff):
        return np.where(np.abs(diff) <= 4, gain[np.clip(diff, -4, 4) + 4], 0.0)

    lane = np.arange(128)
    x, y = lane // 32, lane % 32
    dx = x[:, None] - x[None, :]
    dy = y[:, None] - y[None, :]
    same_y = (dy == 0).astype(np.float64)
    same_x = (dx == 0).astype(np.float64)
    block = np.concatenate(
        [at(dx) * same_y, at(dx - 4) * same_y, at(dx + 4) * same_y, at(dy) * same_x], axis=1
    )
    return np.concatenate([block, block], axis=0)


def split(rows):
    hi = rows.astype(BF16)
    lo = (rows - hi.astype(F32)).astype(BF16)
    return jnp.concatenate([hi, lo], axis=1)


def kernel(
    ap_row, pr_row, source, wavelet, receivers, wave_in, lam_in, mu_in, buoy_in, grad_in, weights_in,
    o_planes, o_owner, o_trace,
    wave, mats, grad, weights, T, RW, TM, G, M, RM, GG, MO,
    PRM, PRO, PR, SZ, SO, V, B, L, MU, MU2, SRC, IMG, HR, QB, QR, R1, L2, TRB, TRS, TRR, OB,
    i_sem, w_send, w_recv, m_send, m_recv, n_send, n_recv, g_send, g_recv, h_send, h_recv,
    p_send, p_recv, halo_send, halo_recv, b_send, b_recv, t_send, t_recv, o_send, o_recv,
):
    s_i = lax.axis_index("shot")
    t_i = lax.axis_index("tile")

    core = s_i % 2
    base = s_i - core
    x_lo = t_i // 4
    d = 2 * (t_i % 4) + core
    role = base + x_lo
    swapped = core != x_lo

    def owner_of(shot, slab):
        return (shot - shot % 2 + slab % 2, (shot % 2) * 4 + slab // 2)

    piece = (s_i + 2 * t_i) % 16
    piece_d = piece // 2
    half = piece % 2
    elsewhere = piece_d != d
    has_left = d > 0
    has_right = d < 7
    left_id = owner_of(role, jnp.maximum(d - 1, 0))
    right_id = owner_of(role, jnp.minimum(d + 1, 7))

    def remote(src, dst, send, recv, device):
        return pltpu.make_async_remote_copy(
            src_ref=src, dst_ref=dst, send_sem=send, recv_sem=recv, device_id=device, device_id_type=MESH
        )

    loads = [
        pltpu.make_async_copy(src, dst, i_sem.at[i])
        for i, (src, dst) in enumerate(
            (
                (lam_in, mats.at[0]),
                (mu_in, mats.at[1]),
                (buoy_in, mats.at[2]),
                (wave_in, wave),
                (grad_in, grad),
                (weights_in, weights),
            )
        )
    ]
    for load in loads:
        load.start()

    barrier = pltpu.get_barrier_semaphore()

    def hello(shot, tile):
        pl.semaphore_signal(barrier, inc=1, device_id=(shot, tile), device_id_type=MESH)

    for k in range(1, 16):
        hello((s_i + k) % 16, t_i)
    for k in range(1, 8):
        for c in range(2):
            hello(base + c, (t_i + k) % 8)

    @pl.when(elsewhere)
    def _():
        hello((2 * d + half - 2 * t_i + 16) % 16, t_i)

    for k in range(8):
        tile = (t_i + k) % 8
        for c in range(2):
            if k + c:
                hello((2 * d + (half + c) % 2 - 2 * tile + 16) % 16, tile)

    for m in range(3):
        loads[m].wait()
        TM[m] = mats[m].T
    loads[3].wait()
    for f in range(9):
        T[f] = wave[f].T
    loads[4].wait()
    loads[5].wait()

    for n in range(STEPS):
        PRM[n : n + 1, :] = jnp.full((1, 128), wavelet[0, n], F32)
    for part in range(2):
        PRM[16 + part : 17 + part, :] = receivers[:, 128 * part : 128 * part + 128].astype(F32)
    PRM[18:19, :] = jnp.full((1, 128), source[0], jnp.int32).astype(F32)

    SZ[:, 0:4] = jnp.zeros((3, 4, 8, 128), F32)
    SZ[:, 36:40] = jnp.zeros((3, 4, 8, 128), F32)

    def blank(side):
        for par in range(2):
            HR[par, side] = jnp.zeros((3, 4, 8, 128), F32)
            QR[par, side] = jnp.zeros((3, 4, 8, 128), F32)
        B[36 * side : 36 * side + 4] = jnp.zeros((4, 8, 128), F32)

    pl.when(jnp.logical_not(has_left))(lambda: blank(0))
    pl.when(jnp.logical_not(has_right))(lambda: blank(1))

    pl.semaphore_wait(barrier, 15 + 14 + 15 + elsewhere.astype(jnp.int32))

    def spread_material(k):
        p = (s_i + k) % 16
        rows = 16 * ((p + 2 * t_i) % 16)
        return remote(TM.at[:, pl.ds(rows, 16), :], G.at[s_i], m_send.at[k], m_recv, (p, t_i))

    spread = [spread_material(k) for k in range(1, 16)]
    for copy in spread:
        copy.start()
    pltpu.make_async_copy(TM.at[:, pl.ds(16 * piece, 16), :], G.at[s_i], m_recv).start()

    table = remote(PRM, PRO, p_send, p_recv, (base + 1 - core, t_i))
    table.start()

    def move_wave(k):
        dd = (d + k) % 8
        return remote(
            T.at[:, pl.ds(32 * dd, 32), :],
            RW.at[:, pl.ds(32 * t_i, 32), :],
            w_send.at[k],
            w_recv,
            owner_of(s_i, dd),
        )

    waves = [move_wave(k) for k in WAVE_ORDER]
    wave_near = move_wave(0)

    @pl.when(jnp.logical_not(swapped))
    def _():
        for i in (0, 1, 2, 3, 4, 5, 6):
            waves[i].start()

    @pl.when(swapped)
    def _():
        for i in (0, 1, 2):
            waves[i].start()

    pl.when(swapped)(wave_near.start)

    @pl.when(jnp.logical_not(swapped))
    def _():
        pltpu.make_async_copy(
            T.at[:, pl.ds(32 * d, 32), :], RW.at[:, pl.ds(32 * t_i, 32), :], w_recv
        ).start()

    table.wait()

    @pl.when(swapped)
    def _():
        PR[...] = PRO[...]

    @pl.when(jnp.logical_not(swapped))
    def _():
        PR[...] = PRM[...]

    iota = lax.broadcasted_iota(jnp.int32, (128, 128), 1)
    for part in range(2):
        ids = jnp.broadcast_to(PR[16 + part : 17 + part, :], (128, 128)).T.astype(jnp.int32)
        z = ids & 255
        y = (ids >> 8) & 31
        x = ids >> 13
        mine = (z >> 5) == d
        row = (z & 31) * 8 + (x >> 2)
        lane = (x & 3) * 32 + y
        rows = pl.ds(128 * part, 128)
        for j in range(2):
            hit = jnp.logical_and(mine, row == iota + 128 * j)
            R1[rows, 128 * j : 128 * j + 128] = jnp.where(hit, 1.0, 0.0).astype(BF16)
        here = jnp.where(lane == iota, 1.0, 0.0)
        L2[rows, 0:128] = here
        L2[rows, 128:256] = here
    IMG[...] = jnp.zeros((32, 8, 128), F32)

    pltpu.make_async_copy(G, G, m_recv).wait()
    for s in range(16):
        M[s] = G[ap_row[s]]

    def send_material(k):
        s = (role + k) % 16
        return remote(
            M.at[s],
            RM.at[:, pl.ds(32 * t_i + 16 * half, 16), :],
            n_send.at[k],
            n_recv,
            owner_of(s, piece_d),
        )

    deliver = [send_material(k) for k in range(16)]
    for k in range(1, 16):
        deliver[k].start()

    @pl.when(elsewhere)
    def _():
        deliver[0].start()

    @pl.when(jnp.logical_not(elsewhere))
    def _():
        pltpu.make_async_copy(M.at[role], RM.at[:, pl.ds(32 * t_i + 16 * half, 16), :], n_recv).start()


    @pl.when(swapped)
    def _():
        for i in (3, 4, 5, 6):
            waves[i].start()

    pltpu.make_async_copy(RW, RW, w_recv).wait()
    for z in range(32):
        rows = pl.ds(z, 8, stride=32)
        for j, f in enumerate(WITH_Z):
            SZ[j, 4 + z] = RW[f, rows, :]
        for j, f in enumerate(IN_PLANE):
            SO[j, z] = RW[f, rows, :]
        for j, f in enumerate(VELOCITY):
            V[j, 4 + z] = RW[f, rows, :]

    def halo(par, part):
        def one(side, src, dst, device):
            return remote(src, dst, halo_send.at[par, side, part], halo_recv.at[par, side, part], device)

        if part == 0:
            to_left = one(0, SZ.at[:, 4:8], HR.at[par, 1], left_id)
            to_right = one(1, SZ.at[:, 32:36], HR.at[par, 0], right_id)
        else:
            to_left = one(0, QB.at[par, 0], QR.at[par, 1], left_id)
            to_right = one(1, QB.at[par, 1], QR.at[par, 0], right_id)
        return to_left, to_right

    def start_halo(par, part):
        to_left, to_right = halo(par, part)
        pl.when(has_left)(to_left.start)
        pl.when(has_right)(to_right.start)

    def wait_halo(par):
        for part in range(2):
            to_left, to_right = halo(par, part)

            @pl.when(has_left)
            def _():
                to_left.wait_send()
                to_right.wait_recv()

            @pl.when(has_right)
            def _():
                to_right.wait_send()
                to_left.wait_recv()

    start_halo(0, 0)

    pltpu.make_async_copy(RM, RM, n_recv).wait()
    for z in range(32):
        B[4 + z] = RM[2, pl.ds(z, 8, stride=32), :] * (DT * UNIT)

    b_left = remote(B.at[4:8], B.at[36:40], b_send.at[0], b_recv.at[0], left_id)
    b_right = remote(B.at[32:36], B.at[0:4], b_send.at[1], b_recv.at[1], right_id)
    pl.when(has_left)(b_left.start)
    pl.when(has_right)(b_right.start)

    sub = lax.broadcasted_iota(jnp.int32, (8, 128), 0)
    lane = lax.broadcasted_iota(jnp.int32, (8, 128), 1)
    cell = (4 * sub + lane // 32) * 8192 + (lane % 32) * 256 + 32 * d
    where_source = PR[18:19, :].astype(jnp.int32)
    for z in range(32):
        shear = RM[1, pl.ds(z, 8, stride=32), :] * (DT * UNIT)
        L[z] = RM[0, pl.ds(z, 8, stride=32), :] * (DT * UNIT)
        MU[z] = shear
        MU2[z] = 2.0 * shear
        SRC[z] = jnp.where(cell + z == where_source, RM[2, pl.ds(z, 8, stride=32), :] * DT, 0.0)

    first = (sub == 0)[None]
    last = (sub == 7)[None]

    def flat(value):
        return value.reshape(64, 128)

    def along_x(same, before, after):
        down = jnp.where(first, 0.0, pltpu.roll(before.reshape(8, 8, 128), 1, 1))
        up = jnp.where(last, 0.0, pltpu.roll(after.reshape(8, 8, 128), 7, 1))
        return same.reshape(8, 8, 128) + (down + up)

    def along_z(load):
        total = None
        for k in range(1, 5):
            term = WEIGHTS[k - 1] * (load(k) - load(-k))
            total = term if total is None else total + term
        return total

    def velocity(parts, amplitude):
        def take(ref, *index, shift=0):
            got = [ref[index + (pl.ds(z + shift, n),)] for z, n in parts]
            return got[0] if len(got) == 1 else jnp.concatenate(got, axis=0)

        def with_z(j, shift=0):
            return take(SZ, j, shift=4 + shift)

        fields = (take(SO, 0), take(SO, 2), with_z(0), take(SO, 1), with_z(1))
        xs = jnp.concatenate([split(flat(field)) for field in fields[0:3]], axis=0)
        ys = jnp.concatenate([split(flat(field)) for field in fields[3:5]], axis=0)
        px = jnp.dot(xs, weights[...], preferred_element_type=F32)
        py = jnp.dot(ys, weights[:, 384:512], preferred_element_type=F32)

        def x_of(m):
            rows = px[64 * m : 64 * m + 64]
            return along_x(rows[:, 0:128], rows[:, 128:256], rows[:, 256:384])

        def y_of(rows):
            return rows.reshape(8, 8, 128)

        ys = (y_of(px[64:128, 384:512]), y_of(py[0:64]), y_of(py[64:128]))
        gain = take(B, shift=4)
        new = [
            take(V, j, shift=4) + gain * (x_of(j) + ys[j] + along_z(lambda k: with_z(j, k)))
            for j in range(3)
        ]
        new[2] = new[2] + take(SRC) * amplitude
        return new

    def inner_velocity(z0, amplitude):
        new = velocity([(z0, 8)], amplitude)
        for j in range(3):
            V[j, pl.ds(z0 + 4, 8)] = new[j]

    def partial_velocity(par, amplitude):
        new = velocity([(0, 4), (28, 4)], amplitude)
        for j in range(3):
            QB[par, 0, j] = new[j][0:4]
            QB[par, 1, j] = new[j][4:8]

    def complete_velocity(par):
        for j in range(4):
            low = high = None
            for k in range(j + 1, 5):
                term = WEIGHTS[k - 1] * HR[par, 0, :, 4 + j - k]
                low = term if low is None else low + term
            for k in range(4 - j, 5):
                term = WEIGHTS[k - 1] * HR[par, 1, :, j - 4 + k]
                high = term if high is None else high + term
            V[:, 4 + j] = QB[par, 0, :, j] - B[4 + j] * low
            V[:, 32 + j] = QB[par, 1, :, j] + B[32 + j] * high
            low = high = None
            for k in range(4 - j, 5):
                term = WEIGHTS[k - 1] * SZ[:, j + k]
                low = term if low is None else low + term
            for k in range(j + 1, 5):
                term = WEIGHTS[k - 1] * SZ[:, 36 + j - k]
                high = term if high is None else high + term
            V[:, j] = QR[par, 0, :, j] + B[j] * low
            V[:, 36 + j] = QR[par, 1, :, j] - B[36 + j] * high

    def stresses(z0):
        def speed(j, shift=0):
            return V[j, pl.ds(z0 + 4 + shift, 8)]

        rows = jnp.concatenate([split(flat(speed(j))) for j in range(3)], axis=0)
        p = jnp.dot(rows, weights[...], preferred_element_type=F32)

        def x_of(m):
            r = p[64 * m : 64 * m + 64]
            return along_x(r[:, 0:128], r[:, 128:256], r[:, 256:384])

        def y_of(m):
            return p[64 * m : 64 * m + 64, 384:512].reshape(8, 8, 128)

        at = pl.ds(z0, 8)
        wide = pl.ds(z0 + 4, 8)
        shear = MU[at]
        exx = x_of(0)
        eyy = y_of(1)
        ezz = along_z(lambda k: speed(2, k))
        SZ[0, wide] = SZ[0, wide] + shear * (along_z(lambda k: speed(0, k)) + x_of(2))
        SZ[1, wide] = SZ[1, wide] + shear * (along_z(lambda k: speed(1, k)) + y_of(2))
        SO[2, at] = SO[2, at] + shear * (y_of(0) + x_of(1))
        div = exx + eyy + ezz
        bulk = L[at] * div
        twice = MU2[at]
        szz = SZ[2, wide] + (bulk + twice * ezz)
        sxx = SO[0, at] + (bulk + twice * exx)
        syy = SO[1, at] + (bulk + twice * eyy)
        SZ[2, wide] = szz
        SO[0, at] = sxx
        SO[1, at] = syy
        IMG[at] = IMG[at] + div * (sxx + syy + szz)

    def spread_grad(k):
        p = (s_i + k) % 16
        return remote(grad.at[pl.ds(8 * p, 8), :], GG.at[s_i], g_send.at[k], g_recv, (p, t_i))

    grads = [spread_grad(k) for k in range(1, 16)]
    def start_gradients():
        for copy in grads:
            copy.start()
        pltpu.make_async_copy(grad.at[pl.ds(8 * s_i, 8), :], GG.at[s_i], g_recv).start()

    def send_owner(k):
        q = (s_i + k) % 16
        return remote(MO.at[q], o_owner.at[pl.ds(8 * s_i, 8), :], h_send.at[k], h_recv, (q, t_i))

    owners = [send_owner(k) for k in range(1, 16)]

    def gradients():
        pltpu.make_async_copy(GG, GG, g_recv).wait()
        for q in range(16):
            total = jnp.zeros((8, 256), F32)
            for s in range(16):
                total = total + jnp.where(pr_row[s] == q, GG[s], 0.0)
            MO[q] = total
        for copy in owners:
            copy.start()
        pltpu.make_async_copy(MO.at[s_i], o_owner.at[pl.ds(8 * s_i, 8), :], h_recv).start()

    partial_velocity(0, PR[0:1, :])
    start_halo(0, 1)

    @pl.when(has_left)
    def _():
        b_left.wait_send()
        b_right.wait_recv()

    @pl.when(has_right)
    def _():
        b_right.wait_send()
        b_left.wait_recv()

    def send_home(part, k):
        t = 4 * ((t_i // 4 + k // 4) % 2) + (t_i + k) % 4
        fields = pl.ds(0, 3) if part == 0 else pl.ds(3, 7)
        return remote(
            OB.at[fields, pl.ds(32 * t, 32), :],
            o_planes.at[fields, pl.ds(32 * d, 32), :],
            o_send.at[part, k],
            o_recv,
            (role, t),
        )

    homes = [[send_home(part, k) for k in (0, 4, 6, 5, 7, 1, 3, 2)] for part in range(2)]

    def start_home(part):
        for copy in homes[part][1:]:
            copy.start()
        pl.when(swapped)(homes[part][0].start)
        fields = pl.ds(0, 3) if part == 0 else pl.ds(3, 7)

        @pl.when(jnp.logical_not(swapped))
        def _():
            pltpu.make_async_copy(
                OB.at[fields, pl.ds(32 * t_i, 32), :], o_planes.at[fields, pl.ds(32 * d, 32), :], o_recv
            ).start()

    def velocities_home():
        for z in range(32):
            rows = pl.ds(z, 8, stride=32)
            for j, f in enumerate(VELOCITY):
                OB[f, rows, :] = V[j, 4 + z]
        start_home(0)

    def step(n, carry):
        par = lax.rem(n, 2)
        amplitude = PR[pl.ds(n, 1), :]
        for z0 in (4, 12, 20):
            inner_velocity(z0, amplitude)
        wait_halo(par)
        complete_velocity(par)
        pl.when(n == STEPS - 1)(velocities_home)
        for z0 in (0, 24):
            stresses(z0)

        @pl.when(n < STEPS - 1)
        def _():
            start_halo(1 - par, 0)
            partial_velocity(1 - par, PR[pl.ds(n + 1, 1), :])
            start_halo(1 - par, 1)

        for z0 in (8, 16):
            stresses(z0)
        picked = jnp.dot(R1[...], split(V[2, 4:36].reshape(256, 128)), preferred_element_type=F32)
        picked = (picked * L2[...]).astype(BF16)
        TRB[n] = lax.dot_general(
            jnp.ones((8, 256), BF16), picked, (((1,), (1,)), ((), ())), preferred_element_type=F32
        )
        pl.when(n == 1)(start_gradients)
        pl.when(n == 5)(gradients)
        return carry

    lax.fori_loop(0, STEPS, step, 0)

    for n in range(STEPS):
        TRS[n : n + 1, :] = TRB[n, 0:1, :]

    def send_trace(k):
        return remote(TRS, TRR.at[d], t_send.at[k], t_recv, (role, (t_i + k) % 8))

    traces = [send_trace(k) for k in range(8)]
    for copy in traces[1:]:
        copy.start()
    pl.when(swapped)(traces[0].start)

    @pl.when(jnp.logical_not(swapped))
    def _():
        pltpu.make_async_copy(TRS, TRR.at[d], t_recv).start()

    for z in range(32):
        rows = pl.ds(z, 8, stride=32)
        for j, f in enumerate(WITH_Z):
            OB[f, rows, :] = SZ[j, 4 + z]
        for j, f in enumerate(IN_PLANE):
            OB[f, rows, :] = SO[j, z]
        OB[9, rows, :] = IMG[z] * UNIT
    start_home(1)

    for copies in (spread, grads, owners, waves):
        for copy in copies:
            copy.wait_send()
    pl.when(swapped)(wave_near.wait_send)
    for k in range(1, 16):
        deliver[k].wait_send()
    pl.when(elsewhere)(deliver[0].wait_send)
    pltpu.make_async_copy(o_owner, o_owner, h_recv).wait()

    pltpu.make_async_copy(TRR, TRR, t_recv).wait()
    total = TRR[0]
    for j in range(1, 8):
        total = total + TRR[j]
    o_trace[...] = total

    pltpu.make_async_copy(o_planes, o_planes, o_recv).wait()
    for copy in homes[0][1:] + homes[1][1:] + traces[1:]:
        copy.wait_send()

    @pl.when(swapped)
    def _():
        for copy in (homes[0][0], homes[1][0], traces[0]):
            copy.wait_send()


def finish(planes, owner, trace, o_state, o_image, o_owner, o_trace):
    for f in range(9):
        o_state[f] = planes[f].T
    o_image[...] = planes[9].T
    o_owner[...] = owner[...]
    for n in range(STEPS):
        o_trace[n] = trace[n : n + 1, :]


def on_device(
    lame_lambda, lame_mu, buoyancy, aperture_row, wave_state, source_cell, wavelet, receiver_cell,
    prev_row, prev_grad,
):
    weights = jnp.asarray(operators(), BF16)
    vmem = pl.BlockSpec(memory_space=pltpu.VMEM)
    smem = pl.BlockSpec(memory_space=pltpu.SMEM)
    dma = pltpu.SemaphoreType.DMA
    tile = (8, 128)
    planes, owner, trace = pl.pallas_call(
        kernel,
        out_shape=(
            jax.ShapeDtypeStruct((10, 256, 128), F32),
            jax.ShapeDtypeStruct((128, 256), F32),
            jax.ShapeDtypeStruct((STEPS, 256), F32),
        ),
        in_specs=[smem] * 4 + [vmem] + [pl.BlockSpec(memory_space=pl.ANY)] * 6,
        out_specs=(pl.BlockSpec(memory_space=pl.ANY), vmem, vmem),
        scratch_shapes=[
            pltpu.VMEM((9, 128, 256), F32),
            pltpu.VMEM((3, 128, 256), F32),
            pltpu.VMEM((128, 256), F32),
            pltpu.VMEM((256, 512), BF16),
            pltpu.VMEM((9, 256, 128), F32),
            pltpu.VMEM((9, 256, 128), F32),
            pltpu.VMEM((3, 256, 128), F32),
            pltpu.VMEM((16, 3, 16, 128), F32),
            pltpu.VMEM((16, 3, 16, 128), F32),
            pltpu.VMEM((3, 256, 128), F32),
            pltpu.VMEM((16, 8, 256), F32),
            pltpu.VMEM((16, 8, 256), F32),
            pltpu.VMEM((24, 128), F32),
            pltpu.VMEM((24, 128), F32),
            pltpu.VMEM((24, 128), F32),
            pltpu.VMEM((3, 40) + tile, F32),
            pltpu.VMEM((3, 32) + tile, F32),
            pltpu.VMEM((3, 40) + tile, F32),
            pltpu.VMEM((40,) + tile, F32),
            pltpu.VMEM((32,) + tile, F32),
            pltpu.VMEM((32,) + tile, F32),
            pltpu.VMEM((32,) + tile, F32),
            pltpu.VMEM((32,) + tile, F32),
            pltpu.VMEM((32,) + tile, F32),
            pltpu.VMEM((2, 2, 3, 4) + tile, F32),
            pltpu.VMEM((2, 2, 3, 4) + tile, F32),
            pltpu.VMEM((2, 2, 3, 4) + tile, F32),
            pltpu.VMEM((256, 256), BF16),
            pltpu.VMEM((256, 256), F32),
            pltpu.VMEM((STEPS, 8, 256), F32),
            pltpu.VMEM((STEPS, 256), F32),
            pltpu.VMEM((8, STEPS, 256), F32),
            pltpu.VMEM((10, 256, 128), F32),
            dma((6,)), dma((8,)), dma, dma((16,)), dma, dma((16,)), dma, dma((16,)), dma, dma((16,)), dma,
            dma, dma, dma((2, 2, 2)), dma((2, 2, 2)), dma((2,)), dma((2,)), dma((8,)), dma, dma((2, 8)), dma,
        ],
        compiler_params=pltpu.CompilerParams(collective_id=0, has_side_effects=True),
        name="wave",
    )(
        aperture_row,
        prev_row,
        source_cell,
        wavelet,
        receiver_cell,
        wave_state.reshape(9, 128, 256),
        lame_lambda.reshape(128, 256),
        lame_mu.reshape(128, 256),
        buoyancy.reshape(128, 256),
        prev_grad.reshape(128, 256),
        weights,
    )
    state, image, owner, trace = pl.pallas_call(
        finish,
        out_shape=(
            jax.ShapeDtypeStruct((9, 128, 256), F32),
            jax.ShapeDtypeStruct((128, 256), F32),
            jax.ShapeDtypeStruct((128, 256), F32),
            jax.ShapeDtypeStruct((STEPS, 1, 256), F32),
        ),
        in_specs=[vmem] * 3,
        out_specs=(vmem,) * 4,
        name="finish",
    )(planes, owner, trace)
    return (
        state.reshape(1, 9, 4, 32, 256),
        image.reshape(1, 4, 32, 256),
        owner.reshape(4, 32, 256),
        jnp.transpose(trace, (1, 0, 2)),
    )


def solution(mesh):
    placed = (
        P(("shot", "tile"), None, None),
        P(("shot", "tile"), None, None),
        P(("shot", "tile"), None, None),
        P(),
        P("shot", None, "tile", None, None),
        P("shot"),
        P("shot", None),
        P("shot", None),
        P(),
        P("shot", "tile", None, None),
    )
    return jax.shard_map(
        on_device,
        mesh=mesh,
        in_specs=placed,
        out_specs=(
            P("shot", None, "tile", None, None),
            P("shot", "tile", None, None),
            P(("shot", "tile"), None, None),
            P("shot", None, None),
        ),
        check_vma=False,
    )
```

```python
import jax
import jax.numpy as jnp
import numpy as np
from jax import lax
from jax.experimental import pallas as pl
from jax.experimental.pallas import tpu as pltpu
from jax.sharding import PartitionSpec as P

MESH = pl.DeviceIdType.MESH
F32 = jnp.float32
BF16 = jnp.bfloat16

WEIGHTS = (672.0, -168.0, 32.0, -3.0)
UNIT = 1.0 / 840.0
DT = 0.2
STEPS = 12

WAVE_ORDER = (1, 3, 2, 4, 5, 7, 6)

VELOCITY = (0, 1, 2)
WITH_Z = (7, 8, 5)
IN_PLANE = (3, 4, 6)


def operators():
    gain = np.zeros(9)
    for k in range(1, 5):
        gain[4 + k] = WEIGHTS[k - 1]
        gain[4 - k] = -WEIGHTS[k - 1]

    def at(diff):
        return np.where(np.abs(diff) <= 4, gain[np.clip(diff, -4, 4) + 4], 0.0)

    lane = np.arange(128)
    x, y = lane // 32, lane % 32
    dx = x[:, None] - x[None, :]
    dy = y[:, None] - y[None, :]
    same_y = (dy == 0).astype(np.float64)
    same_x = (dx == 0).astype(np.float64)
    block = np.concatenate(
        [at(dx) * same_y, at(dx - 4) * same_y, at(dx + 4) * same_y, at(dy) * same_x], axis=1
    )
    return np.concatenate([block, block], axis=0)


def split(rows):
    hi = rows.astype(BF16)
    lo = (rows - hi.astype(F32)).astype(BF16)
    return jnp.concatenate([hi, lo], axis=1)


def kernel(
    ap_row, pr_row, source, wavelet, receivers, wave_in, lam_in, mu_in, buoy_in, grad_in, weights_in,
    o_planes, o_owner, o_trace,
    wave, mats, grad, weights, T, RW, TM, G, M, RM, GG, MO,
    PRM, PRO, PR, SZ, SO, V, B, L, MU, MU2, SRC, IMG, HR, QB, QR, R1, L2, TRB, TRS, TRR, OB,
    i_sem, w_send, w_recv, m_send, m_recv, n_send, n_recv, g_send, g_recv, h_send, h_recv,
    p_send, p_recv, halo_send, halo_recv, b_send, b_recv, t_send, t_recv, o_send, o_recv,
):
    s_i = lax.axis_index("shot")
    t_i = lax.axis_index("tile")

    core = s_i % 2
    base = s_i - core
    x_lo = t_i // 4
    d = 2 * (t_i % 4) + core
    role = base + x_lo
    swapped = core != x_lo

    def owner_of(shot, slab):
        return (shot - shot % 2 + slab % 2, (shot % 2) * 4 + slab // 2)

    piece = (s_i + 2 * t_i) % 16
    piece_d = piece // 2
    half = piece % 2
    elsewhere = piece_d != d
    has_left = d > 0
    has_right = d < 7
    left_id = owner_of(role, jnp.maximum(d - 1, 0))
    right_id = owner_of(role, jnp.minimum(d + 1, 7))

    def remote(src, dst, send, recv, device):
        return pltpu.make_async_remote_copy(
            src_ref=src, dst_ref=dst, send_sem=send, recv_sem=recv, device_id=device, device_id_type=MESH
        )

    loads = [
        pltpu.make_async_copy(src, dst, i_sem.at[i])
        for i, (src, dst) in enumerate(
            (
                (lam_in, mats.at[0]),
                (mu_in, mats.at[1]),
                (buoy_in, mats.at[2]),
                (wave_in, wave),
                (grad_in, grad),
                (weights_in, weights),
            )
        )
    ]
    for load in loads:
        load.start()

    barrier = pltpu.get_barrier_semaphore()

    def hello(shot, tile):
        pl.semaphore_signal(barrier, inc=1, device_id=(shot, tile), device_id_type=MESH)

    for k in range(1, 16):
        hello((s_i + k) % 16, t_i)
    for k in range(1, 8):
        for c in range(2):
            hello(base + c, (t_i + k) % 8)

    @pl.when(elsewhere)
    def _():
        hello((2 * d + half - 2 * t_i + 16) % 16, t_i)

    for k in range(8):
        tile = (t_i + k) % 8
        for c in range(2):
            if k + c:
                hello((2 * d + (half + c) % 2 - 2 * tile + 16) % 16, tile)

    for m in range(3):
        loads[m].wait()
        TM[m] = mats[m].T
    loads[3].wait()
    for f in range(9):
        T[f] = wave[f].T
    loads[4].wait()
    loads[5].wait()

    for n in range(STEPS):
        PRM[n : n + 1, :] = jnp.full((1, 128), wavelet[0, n], F32)
    for part in range(2):
        PRM[16 + part : 17 + part, :] = receivers[:, 128 * part : 128 * part + 128].astype(F32)
    PRM[18:19, :] = jnp.full((1, 128), source[0], jnp.int32).astype(F32)

    SZ[:, 0:4] = jnp.zeros((3, 4, 8, 128), F32)
    SZ[:, 36:40] = jnp.zeros((3, 4, 8, 128), F32)

    def blank(side):
        for par in range(2):
            HR[par, side] = jnp.zeros((3, 4, 8, 128), F32)
            QR[par, side] = jnp.zeros((3, 4, 8, 128), F32)
        B[36 * side : 36 * side + 4] = jnp.zeros((4, 8, 128), F32)

    pl.when(jnp.logical_not(has_left))(lambda: blank(0))
    pl.when(jnp.logical_not(has_right))(lambda: blank(1))

    pl.semaphore_wait(barrier, 15 + 14 + 15 + elsewhere.astype(jnp.int32))

    def spread_material(k):
        p = (s_i + k) % 16
        rows = 16 * ((p + 2 * t_i) % 16)
        return remote(TM.at[:, pl.ds(rows, 16), :], G.at[s_i], m_send.at[k], m_recv, (p, t_i))

    spread = [spread_material(k) for k in range(1, 16)]
    for copy in spread:
        copy.start()
    pltpu.make_async_copy(TM.at[:, pl.ds(16 * piece, 16), :], G.at[s_i], m_recv).start()

    table = remote(PRM, PRO, p_send, p_recv, (base + 1 - core, t_i))
    table.start()

    def move_wave(k):
        dd = (d + k) % 8
        return remote(
            T.at[:, pl.ds(32 * dd, 32), :],
            RW.at[:, pl.ds(32 * t_i, 32), :],
            w_send.at[k],
            w_recv,
            owner_of(s_i, dd),
        )

    waves = [move_wave(k) for k in WAVE_ORDER]
    wave_near = move_wave(0)

    @pl.when(jnp.logical_not(swapped))
    def _():
        for i in (0, 1, 2, 3, 4, 5, 6):
            waves[i].start()

    @pl.when(swapped)
    def _():
        for i in (0, 1, 2):
            waves[i].start()

    pl.when(swapped)(wave_near.start)

    @pl.when(jnp.logical_not(swapped))
    def _():
        pltpu.make_async_copy(
            T.at[:, pl.ds(32 * d, 32), :], RW.at[:, pl.ds(32 * t_i, 32), :], w_recv
        ).start()

    table.wait()

    @pl.when(swapped)
    def _():
        PR[...] = PRO[...]

    @pl.when(jnp.logical_not(swapped))
    def _():
        PR[...] = PRM[...]

    iota = lax.broadcasted_iota(jnp.int32, (128, 128), 1)
    for part in range(2):
        ids = jnp.broadcast_to(PR[16 + part : 17 + part, :], (128, 128)).T.astype(jnp.int32)
        z = ids & 255
        y = (ids >> 8) & 31
        x = ids >> 13
        mine = (z >> 5) == d
        row = (z & 31) * 8 + (x >> 2)
        lane = (x & 3) * 32 + y
        rows = pl.ds(128 * part, 128)
        for j in range(2):
            hit = jnp.logical_and(mine, row == iota + 128 * j)
            R1[rows, 128 * j : 128 * j + 128] = jnp.where(hit, 1.0, 0.0).astype(BF16)
        here = jnp.where(lane == iota, 1.0, 0.0)
        L2[rows, 0:128] = here
        L2[rows, 128:256] = here
    IMG[...] = jnp.zeros((32, 8, 128), F32)

    pltpu.make_async_copy(G, G, m_recv).wait()
    for s in range(16):
        M[s] = G[ap_row[s]]

    def send_material(k):
        s = (role + k) % 16
        return remote(
            M.at[s],
            RM.at[:, pl.ds(32 * t_i + 16 * half, 16), :],
            n_send.at[k],
            n_recv,
            owner_of(s, piece_d),
        )

    deliver = [send_material(k) for k in range(16)]
    for k in range(1, 16):
        deliver[k].start()

    @pl.when(elsewhere)
    def _():
        deliver[0].start()

    @pl.when(jnp.logical_not(elsewhere))
    def _():
        pltpu.make_async_copy(M.at[role], RM.at[:, pl.ds(32 * t_i + 16 * half, 16), :], n_recv).start()


    @pl.when(swapped)
    def _():
        for i in (3, 4, 5, 6):
            waves[i].start()

    pltpu.make_async_copy(RW, RW, w_recv).wait()
    for z in range(32):
        rows = pl.ds(z, 8, stride=32)
        for j, f in enumerate(WITH_Z):
            SZ[j, 4 + z] = RW[f, rows, :]
        for j, f in enumerate(IN_PLANE):
            SO[j, z] = RW[f, rows, :]

    def halo(par, part):
        def one(side, src, dst, device):
            return remote(src, dst, halo_send.at[par, side, part], halo_recv.at[par, side, part], device)

        if part == 0:
            to_left = one(0, SZ.at[:, 4:8], HR.at[par, 1], left_id)
            to_right = one(1, SZ.at[:, 32:36], HR.at[par, 0], right_id)
        else:
            to_left = one(0, QB.at[par, 0], QR.at[par, 1], left_id)
            to_right = one(1, QB.at[par, 1], QR.at[par, 0], right_id)
        return to_left, to_right

    def start_halo(par, part):
        to_left, to_right = halo(par, part)
        pl.when(has_left)(to_left.start)
        pl.when(has_right)(to_right.start)

    def wait_halo(par):
        for part in range(2):
            to_left, to_right = halo(par, part)

            @pl.when(has_left)
            def _():
                to_left.wait_send()
                to_right.wait_recv()

            @pl.when(has_right)
            def _():
                to_right.wait_send()
                to_left.wait_recv()

    start_halo(0, 0)
    for z in range(32):
        for j, f in enumerate(VELOCITY):
            V[j, 4 + z] = RW[f, pl.ds(z, 8, stride=32), :]

    pltpu.make_async_copy(RM, RM, n_recv).wait()
    for z in range(32):
        B[4 + z] = RM[2, pl.ds(z, 8, stride=32), :] * (DT * UNIT)

    b_left = remote(B.at[4:8], B.at[36:40], b_send.at[0], b_recv.at[0], left_id)
    b_right = remote(B.at[32:36], B.at[0:4], b_send.at[1], b_recv.at[1], right_id)
    pl.when(has_left)(b_left.start)
    pl.when(has_right)(b_right.start)

    sub = lax.broadcasted_iota(jnp.int32, (8, 128), 0)
    lane = lax.broadcasted_iota(jnp.int32, (8, 128), 1)
    cell = (4 * sub + lane // 32) * 8192 + (lane % 32) * 256 + 32 * d
    where_source = PR[18:19, :].astype(jnp.int32)
    for z in range(32):
        SRC[z] = jnp.where(cell + z == where_source, RM[2, pl.ds(z, 8, stride=32), :] * DT, 0.0)

    first = (sub == 0)[None]
    last = (sub == 7)[None]

    def flat(value):
        return value.reshape(64, 128)

    def along_x(same, before, after):
        down = jnp.where(first, 0.0, pltpu.roll(before.reshape(8, 8, 128), 1, 1))
        up = jnp.where(last, 0.0, pltpu.roll(after.reshape(8, 8, 128), 7, 1))
        return same.reshape(8, 8, 128) + (down + up)

    def along_z(load):
        total = None
        for k in range(1, 5):
            term = WEIGHTS[k - 1] * (load(k) - load(-k))
            total = term if total is None else total + term
        return total

    def velocity(parts, amplitude):
        def take(ref, *index, shift=0):
            got = [ref[index + (pl.ds(z + shift, n),)] for z, n in parts]
            return got[0] if len(got) == 1 else jnp.concatenate(got, axis=0)

        def with_z(j, shift=0):
            return take(SZ, j, shift=4 + shift)

        fields = (take(SO, 0), take(SO, 2), with_z(0), take(SO, 1), with_z(1))
        xs = jnp.concatenate([split(flat(field)) for field in fields[0:3]], axis=0)
        ys = jnp.concatenate([split(flat(field)) for field in fields[3:5]], axis=0)
        px = jnp.dot(xs, weights[...], preferred_element_type=F32)
        py = jnp.dot(ys, weights[:, 384:512], preferred_element_type=F32)

        def x_of(m):
            rows = px[64 * m : 64 * m + 64]
            return along_x(rows[:, 0:128], rows[:, 128:256], rows[:, 256:384])

        def y_of(rows):
            return rows.reshape(8, 8, 128)

        ys = (y_of(px[64:128, 384:512]), y_of(py[0:64]), y_of(py[64:128]))
        gain = take(B, shift=4)
        new = [
            take(V, j, shift=4) + gain * (x_of(j) + ys[j] + along_z(lambda k: with_z(j, k)))
            for j in range(3)
        ]
        new[2] = new[2] + take(SRC) * amplitude
        return new

    def inner_velocity(z0, amplitude):
        new = velocity([(z0, 8)], amplitude)
        for j in range(3):
            V[j, pl.ds(z0 + 4, 8)] = new[j]

    def partial_velocity(par, amplitude):
        new = velocity([(0, 4), (28, 4)], amplitude)
        for j in range(3):
            QB[par, 0, j] = new[j][0:4]
            QB[par, 1, j] = new[j][4:8]

    def complete_velocity(par):
        for j in range(4):
            low = high = None
            for k in range(j + 1, 5):
                term = WEIGHTS[k - 1] * HR[par, 0, :, 4 + j - k]
                low = term if low is None else low + term
            for k in range(4 - j, 5):
                term = WEIGHTS[k - 1] * HR[par, 1, :, j - 4 + k]
                high = term if high is None else high + term
            V[:, 4 + j] = QB[par, 0, :, j] - B[4 + j] * low
            V[:, 32 + j] = QB[par, 1, :, j] + B[32 + j] * high
            low = high = None
            for k in range(4 - j, 5):
                term = WEIGHTS[k - 1] * SZ[:, j + k]
                low = term if low is None else low + term
            for k in range(j + 1, 5):
                term = WEIGHTS[k - 1] * SZ[:, 36 + j - k]
                high = term if high is None else high + term
            V[:, j] = QR[par, 0, :, j] + B[j] * low
            V[:, 36 + j] = QR[par, 1, :, j] - B[36 + j] * high

    def stresses(z0):
        def speed(j, shift=0):
            return V[j, pl.ds(z0 + 4 + shift, 8)]

        rows = jnp.concatenate([split(flat(speed(j))) for j in range(3)], axis=0)
        p = jnp.dot(rows, weights[...], preferred_element_type=F32)

        def x_of(m):
            r = p[64 * m : 64 * m + 64]
            return along_x(r[:, 0:128], r[:, 128:256], r[:, 256:384])

        def y_of(m):
            return p[64 * m : 64 * m + 64, 384:512].reshape(8, 8, 128)

        at = pl.ds(z0, 8)
        wide = pl.ds(z0 + 4, 8)
        shear = MU[at]
        exx = x_of(0)
        eyy = y_of(1)
        ezz = along_z(lambda k: speed(2, k))
        SZ[0, wide] = SZ[0, wide] + shear * (along_z(lambda k: speed(0, k)) + x_of(2))
        SZ[1, wide] = SZ[1, wide] + shear * (along_z(lambda k: speed(1, k)) + y_of(2))
        SO[2, at] = SO[2, at] + shear * (y_of(0) + x_of(1))
        div = exx + eyy + ezz
        bulk = L[at] * div
        twice = MU2[at]
        szz = SZ[2, wide] + (bulk + twice * ezz)
        sxx = SO[0, at] + (bulk + twice * exx)
        syy = SO[1, at] + (bulk + twice * eyy)
        SZ[2, wide] = szz
        SO[0, at] = sxx
        SO[1, at] = syy
        IMG[at] = IMG[at] + div * (sxx + syy + szz)

    def spread_grad(k):
        p = (s_i + k) % 16
        return remote(grad.at[pl.ds(8 * p, 8), :], GG.at[s_i], g_send.at[k], g_recv, (p, t_i))

    grads = [spread_grad(k) for k in range(1, 16)]
    def start_gradients():
        for copy in grads:
            copy.start()
        pltpu.make_async_copy(grad.at[pl.ds(8 * s_i, 8), :], GG.at[s_i], g_recv).start()

    def send_owner(k):
        q = (s_i + k) % 16
        return remote(MO.at[q], o_owner.at[pl.ds(8 * s_i, 8), :], h_send.at[k], h_recv, (q, t_i))

    owners = [send_owner(k) for k in range(1, 16)]

    def gradients():
        pltpu.make_async_copy(GG, GG, g_recv).wait()
        for q in range(16):
            total = jnp.zeros((8, 256), F32)
            for s in range(16):
                total = total + jnp.where(pr_row[s] == q, GG[s], 0.0)
            MO[q] = total
        for copy in owners:
            copy.start()
        pltpu.make_async_copy(MO.at[s_i], o_owner.at[pl.ds(8 * s_i, 8), :], h_recv).start()

    partial_velocity(0, PR[0:1, :])
    start_halo(0, 1)
    for z in range(32):
        shear = RM[1, pl.ds(z, 8, stride=32), :] * (DT * UNIT)
        L[z] = RM[0, pl.ds(z, 8, stride=32), :] * (DT * UNIT)
        MU[z] = shear
        MU2[z] = 2.0 * shear

    @pl.when(has_left)
    def _():
        b_left.wait_send()
        b_right.wait_recv()

    @pl.when(has_right)
    def _():
        b_right.wait_send()
        b_left.wait_recv()

    def send_home(part, k):
        t = 4 * ((t_i // 4 + k // 4) % 2) + (t_i + k) % 4
        fields = pl.ds(0, 3) if part == 0 else pl.ds(3, 7)
        return remote(
            OB.at[fields, pl.ds(32 * t, 32), :],
            o_planes.at[fields, pl.ds(32 * d, 32), :],
            o_send.at[part, k],
            o_recv,
            (role, t),
        )

    homes = [[send_home(part, k) for k in (0, 4, 6, 5, 7, 1, 3, 2)] for part in range(2)]

    def start_home(part):
        for copy in homes[part][1:]:
            copy.start()
        pl.when(swapped)(homes[part][0].start)
        fields = pl.ds(0, 3) if part == 0 else pl.ds(3, 7)

        @pl.when(jnp.logical_not(swapped))
        def _():
            pltpu.make_async_copy(
                OB.at[fields, pl.ds(32 * t_i, 32), :], o_planes.at[fields, pl.ds(32 * d, 32), :], o_recv
            ).start()

    def velocities_home():
        for z in range(32):
            rows = pl.ds(z, 8, stride=32)
            for j, f in enumerate(VELOCITY):
                OB[f, rows, :] = V[j, 4 + z]
        start_home(0)

    def step(n, carry):
        par = lax.rem(n, 2)
        amplitude = PR[pl.ds(n, 1), :]
        for z0 in (4, 12, 20):
            inner_velocity(z0, amplitude)
        wait_halo(par)
        complete_velocity(par)
        pl.when(n == STEPS - 1)(velocities_home)
        for z0 in (0, 24):
            stresses(z0)

        @pl.when(n < STEPS - 1)
        def _():
            start_halo(1 - par, 0)
            partial_velocity(1 - par, PR[pl.ds(n + 1, 1), :])
            start_halo(1 - par, 1)

        for z0 in (8, 16):
            stresses(z0)
        picked = jnp.dot(R1[...], split(V[2, 4:36].reshape(256, 128)), preferred_element_type=F32)
        picked = (picked * L2[...]).astype(BF16)
        TRB[n] = lax.dot_general(
            jnp.ones((8, 256), BF16), picked, (((1,), (1,)), ((), ())), preferred_element_type=F32
        )
        pl.when(n == 1)(start_gradients)
        pl.when(n == 5)(gradients)
        return carry

    lax.fori_loop(0, STEPS, step, 0)

    for n in range(STEPS):
        TRS[n : n + 1, :] = TRB[n, 0:1, :]

    def send_trace(k):
        return remote(TRS, TRR.at[d], t_send.at[k], t_recv, (role, (t_i + k) % 8))

    traces = [send_trace(k) for k in range(8)]
    for copy in traces[1:]:
        copy.start()
    pl.when(swapped)(traces[0].start)

    @pl.when(jnp.logical_not(swapped))
    def _():
        pltpu.make_async_copy(TRS, TRR.at[d], t_recv).start()

    for z in range(32):
        rows = pl.ds(z, 8, stride=32)
        for j, f in enumerate(WITH_Z):
            OB[f, rows, :] = SZ[j, 4 + z]
        for j, f in enumerate(IN_PLANE):
            OB[f, rows, :] = SO[j, z]
        OB[9, rows, :] = IMG[z] * UNIT
    start_home(1)

    for copies in (spread, grads, owners, waves):
        for copy in copies:
            copy.wait_send()
    pl.when(swapped)(wave_near.wait_send)
    for k in range(1, 16):
        deliver[k].wait_send()
    pl.when(elsewhere)(deliver[0].wait_send)
    pltpu.make_async_copy(o_owner, o_owner, h_recv).wait()

    pltpu.make_async_copy(TRR, TRR, t_recv).wait()
    total = TRR[0]
    for j in range(1, 8):
        total = total + TRR[j]
    o_trace[...] = total

    pltpu.make_async_copy(o_planes, o_planes, o_recv).wait()
    for copy in homes[0][1:] + homes[1][1:] + traces[1:]:
        copy.wait_send()

    @pl.when(swapped)
    def _():
        for copy in (homes[0][0], homes[1][0], traces[0]):
            copy.wait_send()


def finish(planes, owner, trace, o_state, o_image, o_owner, o_trace):
    for f in range(9):
        o_state[f] = planes[f].T
    o_image[...] = planes[9].T
    o_owner[...] = owner[...]
    for n in range(STEPS):
        o_trace[n] = trace[n : n + 1, :]


def on_device(
    lame_lambda, lame_mu, buoyancy, aperture_row, wave_state, source_cell, wavelet, receiver_cell,
    prev_row, prev_grad,
):
    weights = jnp.asarray(operators(), BF16)
    vmem = pl.BlockSpec(memory_space=pltpu.VMEM)
    smem = pl.BlockSpec(memory_space=pltpu.SMEM)
    dma = pltpu.SemaphoreType.DMA
    tile = (8, 128)
    planes, owner, trace = pl.pallas_call(
        kernel,
        out_shape=(
            jax.ShapeDtypeStruct((10, 256, 128), F32),
            jax.ShapeDtypeStruct((128, 256), F32),
            jax.ShapeDtypeStruct((STEPS, 256), F32),
        ),
        in_specs=[smem] * 4 + [vmem] + [pl.BlockSpec(memory_space=pl.ANY)] * 6,
        out_specs=(pl.BlockSpec(memory_space=pl.ANY), vmem, vmem),
        scratch_shapes=[
            pltpu.VMEM((9, 128, 256), F32),
            pltpu.VMEM((3, 128, 256), F32),
            pltpu.VMEM((128, 256), F32),
            pltpu.VMEM((256, 512), BF16),
            pltpu.VMEM((9, 256, 128), F32),
            pltpu.VMEM((9, 256, 128), F32),
            pltpu.VMEM((3, 256, 128), F32),
            pltpu.VMEM((16, 3, 16, 128), F32),
            pltpu.VMEM((16, 3, 16, 128), F32),
            pltpu.VMEM((3, 256, 128), F32),
            pltpu.VMEM((16, 8, 256), F32),
            pltpu.VMEM((16, 8, 256), F32),
            pltpu.VMEM((24, 128), F32),
            pltpu.VMEM((24, 128), F32),
            pltpu.VMEM((24, 128), F32),
            pltpu.VMEM((3, 40) + tile, F32),
            pltpu.VMEM((3, 32) + tile, F32),
            pltpu.VMEM((3, 40) + tile, F32),
            pltpu.VMEM((40,) + tile, F32),
            pltpu.VMEM((32,) + tile, F32),
            pltpu.VMEM((32,) + tile, F32),
            pltpu.VMEM((32,) + tile, F32),
            pltpu.VMEM((32,) + tile, F32),
            pltpu.VMEM((32,) + tile, F32),
            pltpu.VMEM((2, 2, 3, 4) + tile, F32),
            pltpu.VMEM((2, 2, 3, 4) + tile, F32),
            pltpu.VMEM((2, 2, 3, 4) + tile, F32),
            pltpu.VMEM((256, 256), BF16),
            pltpu.VMEM((256, 256), F32),
            pltpu.VMEM((STEPS, 8, 256), F32),
            pltpu.VMEM((STEPS, 256), F32),
            pltpu.VMEM((8, STEPS, 256), F32),
            pltpu.VMEM((10, 256, 128), F32),
            dma((6,)), dma((8,)), dma, dma((16,)), dma, dma((16,)), dma, dma((16,)), dma, dma((16,)), dma,
            dma, dma, dma((2, 2, 2)), dma((2, 2, 2)), dma((2,)), dma((2,)), dma((8,)), dma, dma((2, 8)), dma,
        ],
        compiler_params=pltpu.CompilerParams(collective_id=0, has_side_effects=True),
        name="wave",
    )(
        aperture_row,
        prev_row,
        source_cell,
        wavelet,
        receiver_cell,
        wave_state.reshape(9, 128, 256),
        lame_lambda.reshape(128, 256),
        lame_mu.reshape(128, 256),
        buoyancy.reshape(128, 256),
        prev_grad.reshape(128, 256),
        weights,
    )
    state, image, owner, trace = pl.pallas_call(
        finish,
        out_shape=(
            jax.ShapeDtypeStruct((9, 128, 256), F32),
            jax.ShapeDtypeStruct((128, 256), F32),
            jax.ShapeDtypeStruct((128, 256), F32),
            jax.ShapeDtypeStruct((STEPS, 1, 256), F32),
        ),
        in_specs=[vmem] * 3,
        out_specs=(vmem,) * 4,
        name="finish",
    )(planes, owner, trace)
    return (
        state.reshape(1, 9, 4, 32, 256),
        image.reshape(1, 4, 32, 256),
        owner.reshape(4, 32, 256),
        jnp.transpose(trace, (1, 0, 2)),
    )


def solution(mesh):
    placed = (
        P(("shot", "tile"), None, None),
        P(("shot", "tile"), None, None),
        P(("shot", "tile"), None, None),
        P(),
        P("shot", None, "tile", None, None),
        P("shot"),
        P("shot", None),
        P("shot", None),
        P(),
        P("shot", "tile", None, None),
    )
    return jax.shard_map(
        on_device,
        mesh=mesh,
        in_specs=placed,
        out_specs=(
            P("shot", None, "tile", None, None),
            P("shot", "tile", None, None),
            P(("shot", "tile"), None, None),
            P("shot", None, None),
        ),
        check_vma=False,
    )
```

```python
import jax
import jax.numpy as jnp
import numpy as np
from jax import lax
from jax.experimental import pallas as pl
from jax.experimental.pallas import tpu as pltpu
from jax.sharding import PartitionSpec as P

MESH = pl.DeviceIdType.MESH
F32 = jnp.float32
BF16 = jnp.bfloat16

WEIGHTS = (672.0, -168.0, 32.0, -3.0)
UNIT = 1.0 / 840.0
DT = 0.2
STEPS = 12

WAVE_ORDER = (4, 3, 5, 2, 6, 1, 7)

VELOCITY = (0, 1, 2)
WITH_Z = (7, 8, 5)
IN_PLANE = (3, 4, 6)


def operators():
    gain = np.zeros(9)
    for k in range(1, 5):
        gain[4 + k] = WEIGHTS[k - 1]
        gain[4 - k] = -WEIGHTS[k - 1]

    def at(diff):
        return np.where(np.abs(diff) <= 4, gain[np.clip(diff, -4, 4) + 4], 0.0)

    lane = np.arange(128)
    x, y = lane // 32, lane % 32
    dx = x[:, None] - x[None, :]
    dy = y[:, None] - y[None, :]
    same_y = (dy == 0).astype(np.float64)
    same_x = (dx == 0).astype(np.float64)
    block = np.concatenate(
        [at(dx) * same_y, at(dx - 4) * same_y, at(dx + 4) * same_y, at(dy) * same_x], axis=1
    )
    return np.concatenate([block, block], axis=0)


def split(rows):
    hi = rows.astype(BF16)
    lo = (rows - hi.astype(F32)).astype(BF16)
    return jnp.concatenate([hi, lo], axis=1)


def kernel(
    ap_row, pr_row, source, wavelet, receivers, wave_in, lam_in, mu_in, buoy_in, grad_in, weights_in,
    o_planes, o_owner, o_trace,
    wave, mats, grad, weights, T, RW, TM, G, M, RM, GG, MO,
    PRM, PRO, PR, SZ, SO, V, B, L, MU, MU2, SRC, IMG, HR, QB, QR, R1, L2, TRB, TRS, TRR, OB,
    i_sem, w_send, w_recv, m_send, m_recv, n_send, n_recv, g_send, g_recv, h_send, h_recv,
    p_send, p_recv, halo_send, halo_recv, b_send, b_recv, t_send, t_recv, o_send, o_recv,
):
    s_i = lax.axis_index("shot")
    t_i = lax.axis_index("tile")

    core = s_i % 2
    base = s_i - core
    x_lo = t_i // 4
    d = 2 * (t_i % 4) + core
    role = base + x_lo
    swapped = core != x_lo

    def owner_of(shot, slab):
        return (shot - shot % 2 + slab % 2, (shot % 2) * 4 + slab // 2)

    piece = (s_i + 2 * t_i) % 16
    piece_d = piece // 2
    half = piece % 2
    elsewhere = piece_d != d
    has_left = d > 0
    has_right = d < 7
    left_id = owner_of(role, jnp.maximum(d - 1, 0))
    right_id = owner_of(role, jnp.minimum(d + 1, 7))

    def remote(src, dst, send, recv, device):
        return pltpu.make_async_remote_copy(
            src_ref=src, dst_ref=dst, send_sem=send, recv_sem=recv, device_id=device, device_id_type=MESH
        )

    loads = [
        pltpu.make_async_copy(src, dst, i_sem.at[i])
        for i, (src, dst) in enumerate(
            (
                (lam_in, mats.at[0]),
                (mu_in, mats.at[1]),
                (buoy_in, mats.at[2]),
                (wave_in, wave),
                (grad_in, grad),
                (weights_in, weights),
            )
        )
    ]
    for load in loads:
        load.start()

    barrier = pltpu.get_barrier_semaphore()

    def hello(shot, tile):
        pl.semaphore_signal(barrier, inc=1, device_id=(shot, tile), device_id_type=MESH)

    for k in range(1, 16):
        hello((s_i + k) % 16, t_i)
    for k in range(1, 8):
        for c in range(2):
            hello(base + c, (t_i + k) % 8)

    @pl.when(elsewhere)
    def _():
        hello((2 * d + half - 2 * t_i + 16) % 16, t_i)

    for k in range(8):
        tile = (t_i + k) % 8
        for c in range(2):
            if k + c:
                hello((2 * d + (half + c) % 2 - 2 * tile + 16) % 16, tile)

    for m in range(3):
        loads[m].wait()
        TM[m] = mats[m].T
    loads[3].wait()
    for f in range(9):
        T[f] = wave[f].T
    loads[4].wait()
    loads[5].wait()

    for n in range(STEPS):
        PRM[n : n + 1, :] = jnp.full((1, 128), wavelet[0, n], F32)
    for part in range(2):
        PRM[16 + part : 17 + part, :] = receivers[:, 128 * part : 128 * part + 128].astype(F32)
    PRM[18:19, :] = jnp.full((1, 128), source[0], jnp.int32).astype(F32)

    SZ[:, 0:4] = jnp.zeros((3, 4, 8, 128), F32)
    SZ[:, 36:40] = jnp.zeros((3, 4, 8, 128), F32)

    def blank(side):
        for par in range(2):
            HR[par, side] = jnp.zeros((3, 4, 8, 128), F32)
            QR[par, side] = jnp.zeros((3, 4, 8, 128), F32)
        B[36 * side : 36 * side + 4] = jnp.zeros((4, 8, 128), F32)

    pl.when(jnp.logical_not(has_left))(lambda: blank(0))
    pl.when(jnp.logical_not(has_right))(lambda: blank(1))

    pl.semaphore_wait(barrier, 15 + 14 + 15 + elsewhere.astype(jnp.int32))

    def spread_material(k):
        p = (s_i + k) % 16
        rows = 16 * ((p + 2 * t_i) % 16)
        return remote(TM.at[:, pl.ds(rows, 16), :], G.at[s_i], m_send.at[k], m_recv, (p, t_i))

    spread = [spread_material(k) for k in range(1, 16)]
    for copy in spread:
        copy.start()
    pltpu.make_async_copy(TM.at[:, pl.ds(16 * piece, 16), :], G.at[s_i], m_recv).start()

    table = remote(PRM, PRO, p_send, p_recv, (base + 1 - core, t_i))
    table.start()

    def move_wave(k):
        dd = (d + k) % 8
        return remote(
            T.at[:, pl.ds(32 * dd, 32), :],
            RW.at[:, pl.ds(32 * t_i, 32), :],
            w_send.at[k],
            w_recv,
            owner_of(s_i, dd),
        )

    waves = [move_wave(k) for k in WAVE_ORDER]
    wave_near = move_wave(0)

    @pl.when(jnp.logical_not(swapped))
    def _():
        for i in (0, 1, 2, 3, 4, 5, 6):
            waves[i].start()

    @pl.when(swapped)
    def _():
        for i in (0, 1, 2):
            waves[i].start()

    pl.when(swapped)(wave_near.start)

    @pl.when(jnp.logical_not(swapped))
    def _():
        pltpu.make_async_copy(
            T.at[:, pl.ds(32 * d, 32), :], RW.at[:, pl.ds(32 * t_i, 32), :], w_recv
        ).start()

    table.wait()

    @pl.when(swapped)
    def _():
        PR[...] = PRO[...]

    @pl.when(jnp.logical_not(swapped))
    def _():
        PR[...] = PRM[...]

    iota = lax.broadcasted_iota(jnp.int32, (128, 128), 1)
    for part in range(2):
        ids = jnp.broadcast_to(PR[16 + part : 17 + part, :], (128, 128)).T.astype(jnp.int32)
        z = ids & 255
        y = (ids >> 8) & 31
        x = ids >> 13
        mine = (z >> 5) == d
        row = (z & 31) * 8 + (x >> 2)
        lane = (x & 3) * 32 + y
        rows = pl.ds(128 * part, 128)
        for j in range(2):
            hit = jnp.logical_and(mine, row == iota + 128 * j)
            R1[rows, 128 * j : 128 * j + 128] = jnp.where(hit, 1.0, 0.0).astype(BF16)
        here = jnp.where(lane == iota, 1.0, 0.0)
        L2[rows, 0:128] = here
        L2[rows, 128:256] = here
    IMG[...] = jnp.zeros((32, 8, 128), F32)

    pltpu.make_async_copy(G, G, m_recv).wait()
    for s in range(16):
        M[s] = G[ap_row[s]]

    def send_material(k):
        s = (role + k) % 16
        return remote(
            M.at[s],
            RM.at[:, pl.ds(32 * t_i + 16 * half, 16), :],
            n_send.at[k],
            n_recv,
            owner_of(s, piece_d),
        )

    deliver = [send_material(k) for k in range(16)]
    for k in range(1, 16):
        deliver[k].start()

    @pl.when(elsewhere)
    def _():
        deliver[0].start()

    @pl.when(jnp.logical_not(elsewhere))
    def _():
        pltpu.make_async_copy(M.at[role], RM.at[:, pl.ds(32 * t_i + 16 * half, 16), :], n_recv).start()


    @pl.when(swapped)
    def _():
        for i in (3, 4, 5, 6):
            waves[i].start()

    pltpu.make_async_copy(RW, RW, w_recv).wait()
    for z in range(32):
        rows = pl.ds(z, 8, stride=32)
        for j, f in enumerate(WITH_Z):
            SZ[j, 4 + z] = RW[f, rows, :]
        for j, f in enumerate(IN_PLANE):
            SO[j, z] = RW[f, rows, :]

    def halo(par, part):
        def one(side, src, dst, device):
            return remote(src, dst, halo_send.at[par, side, part], halo_recv.at[par, side, part], device)

        if part == 0:
            to_left = one(0, SZ.at[:, 4:8], HR.at[par, 1], left_id)
            to_right = one(1, SZ.at[:, 32:36], HR.at[par, 0], right_id)
        else:
            to_left = one(0, QB.at[par, 0], QR.at[par, 1], left_id)
            to_right = one(1, QB.at[par, 1], QR.at[par, 0], right_id)
        return to_left, to_right

    def start_halo(par, part):
        to_left, to_right = halo(par, part)
        pl.when(has_left)(to_left.start)
        pl.when(has_right)(to_right.start)

    def wait_halo(par):
        for part in range(2):
            to_left, to_right = halo(par, part)

            @pl.when(has_left)
            def _():
                to_left.wait_send()
                to_right.wait_recv()

            @pl.when(has_right)
            def _():
                to_right.wait_send()
                to_left.wait_recv()

    start_halo(0, 0)
    for z in range(32):
        for j, f in enumerate(VELOCITY):
            V[j, 4 + z] = RW[f, pl.ds(z, 8, stride=32), :]

    pltpu.make_async_copy(RM, RM, n_recv).wait()
    for z in range(32):
        B[4 + z] = RM[2, pl.ds(z, 8, stride=32), :] * (DT * UNIT)

    b_left = remote(B.at[4:8], B.at[36:40], b_send.at[0], b_recv.at[0], left_id)
    b_right = remote(B.at[32:36], B.at[0:4], b_send.at[1], b_recv.at[1], right_id)
    pl.when(has_left)(b_left.start)
    pl.when(has_right)(b_right.start)

    sub = lax.broadcasted_iota(jnp.int32, (8, 128), 0)
    lane = lax.broadcasted_iota(jnp.int32, (8, 128), 1)
    cell = (4 * sub + lane // 32) * 8192 + (lane % 32) * 256 + 32 * d
    where_source = PR[18:19, :].astype(jnp.int32)
    for z in range(32):
        SRC[z] = jnp.where(cell + z == where_source, RM[2, pl.ds(z, 8, stride=32), :] * DT, 0.0)

    first = (sub == 0)[None]
    last = (sub == 7)[None]

    def flat(value):
        return value.reshape(64, 128)

    def along_x(same, before, after):
        down = jnp.where(first, 0.0, pltpu.roll(before.reshape(8, 8, 128), 1, 1))
        up = jnp.where(last, 0.0, pltpu.roll(after.reshape(8, 8, 128), 7, 1))
        return same.reshape(8, 8, 128) + (down + up)

    def along_z(load):
        total = None
        for k in range(1, 5):
            term = WEIGHTS[k - 1] * (load(k) - load(-k))
            total = term if total is None else total + term
        return total

    def velocity(parts, amplitude):
        def take(ref, *index, shift=0):
            got = [ref[index + (pl.ds(z + shift, n),)] for z, n in parts]
            return got[0] if len(got) == 1 else jnp.concatenate(got, axis=0)

        def with_z(j, shift=0):
            return take(SZ, j, shift=4 + shift)

        fields = (take(SO, 0), take(SO, 2), with_z(0), take(SO, 1), with_z(1))
        xs = jnp.concatenate([split(flat(field)) for field in fields[0:3]], axis=0)
        ys = jnp.concatenate([split(flat(field)) for field in fields[3:5]], axis=0)
        px = jnp.dot(xs, weights[...], preferred_element_type=F32)
        py = jnp.dot(ys, weights[:, 384:512], preferred_element_type=F32)

        def x_of(m):
            rows = px[64 * m : 64 * m + 64]
            return along_x(rows[:, 0:128], rows[:, 128:256], rows[:, 256:384])

        def y_of(rows):
            return rows.reshape(8, 8, 128)

        ys = (y_of(px[64:128, 384:512]), y_of(py[0:64]), y_of(py[64:128]))
        gain = take(B, shift=4)
        new = [
            take(V, j, shift=4) + gain * (x_of(j) + ys[j] + along_z(lambda k: with_z(j, k)))
            for j in range(3)
        ]
        new[2] = new[2] + take(SRC) * amplitude
        return new

    def inner_velocity(z0, amplitude):
        new = velocity([(z0, 8)], amplitude)
        for j in range(3):
            V[j, pl.ds(z0 + 4, 8)] = new[j]

    def partial_velocity(par, amplitude):
        new = velocity([(0, 4), (28, 4)], amplitude)
        for j in range(3):
            QB[par, 0, j] = new[j][0:4]
            QB[par, 1, j] = new[j][4:8]

    def complete_velocity(par):
        for j in range(4):
            low = high = None
            for k in range(j + 1, 5):
                term = WEIGHTS[k - 1] * HR[par, 0, :, 4 + j - k]
                low = term if low is None else low + term
            for k in range(4 - j, 5):
                term = WEIGHTS[k - 1] * HR[par, 1, :, j - 4 + k]
                high = term if high is None else high + term
            V[:, 4 + j] = QB[par, 0, :, j] - B[4 + j] * low
            V[:, 32 + j] = QB[par, 1, :, j] + B[32 + j] * high
            low = high = None
            for k in range(4 - j, 5):
                term = WEIGHTS[k - 1] * SZ[:, j + k]
                low = term if low is None else low + term
            for k in range(j + 1, 5):
                term = WEIGHTS[k - 1] * SZ[:, 36 + j - k]
                high = term if high is None else high + term
            V[:, j] = QR[par, 0, :, j] + B[j] * low
            V[:, 36 + j] = QR[par, 1, :, j] - B[36 + j] * high

    def stresses(z0):
        def speed(j, shift=0):
            return V[j, pl.ds(z0 + 4 + shift, 8)]

        rows = jnp.concatenate([split(flat(speed(j))) for j in range(3)], axis=0)
        p = jnp.dot(rows, weights[...], preferred_element_type=F32)

        def x_of(m):
            r = p[64 * m : 64 * m + 64]
            return along_x(r[:, 0:128], r[:, 128:256], r[:, 256:384])

        def y_of(m):
            return p[64 * m : 64 * m + 64, 384:512].reshape(8, 8, 128)

        at = pl.ds(z0, 8)
        wide = pl.ds(z0 + 4, 8)
        shear = MU[at]
        exx = x_of(0)
        eyy = y_of(1)
        ezz = along_z(lambda k: speed(2, k))
        SZ[0, wide] = SZ[0, wide] + shear * (along_z(lambda k: speed(0, k)) + x_of(2))
        SZ[1, wide] = SZ[1, wide] + shear * (along_z(lambda k: speed(1, k)) + y_of(2))
        SO[2, at] = SO[2, at] + shear * (y_of(0) + x_of(1))
        div = exx + eyy + ezz
        bulk = L[at] * div
        twice = MU2[at]
        szz = SZ[2, wide] + (bulk + twice * ezz)
        sxx = SO[0, at] + (bulk + twice * exx)
        syy = SO[1, at] + (bulk + twice * eyy)
        SZ[2, wide] = szz
        SO[0, at] = sxx
        SO[1, at] = syy
        IMG[at] = IMG[at] + div * (sxx + syy + szz)

    def spread_grad(k):
        p = (s_i + k) % 16
        return remote(grad.at[pl.ds(8 * p, 8), :], GG.at[s_i], g_send.at[k], g_recv, (p, t_i))

    grads = [spread_grad(k) for k in range(1, 16)]
    def start_gradients():
        for copy in grads:
            copy.start()
        pltpu.make_async_copy(grad.at[pl.ds(8 * s_i, 8), :], GG.at[s_i], g_recv).start()

    def send_owner(k):
        q = (s_i + k) % 16
        return remote(MO.at[q], o_owner.at[pl.ds(8 * s_i, 8), :], h_send.at[k], h_recv, (q, t_i))

    owners = [send_owner(k) for k in range(1, 16)]

    def gradients():
        pltpu.make_async_copy(GG, GG, g_recv).wait()
        for q in range(16):
            total = jnp.zeros((8, 256), F32)
            for s in range(16):
                total = total + jnp.where(pr_row[s] == q, GG[s], 0.0)
            MO[q] = total
        for copy in owners:
            copy.start()
        pltpu.make_async_copy(MO.at[s_i], o_owner.at[pl.ds(8 * s_i, 8), :], h_recv).start()

    partial_velocity(0, PR[0:1, :])
    start_halo(0, 1)
    for z in range(32):
        shear = RM[1, pl.ds(z, 8, stride=32), :] * (DT * UNIT)
        L[z] = RM[0, pl.ds(z, 8, stride=32), :] * (DT * UNIT)
        MU[z] = shear
        MU2[z] = 2.0 * shear

    @pl.when(has_left)
    def _():
        b_left.wait_send()
        b_right.wait_recv()

    @pl.when(has_right)
    def _():
        b_right.wait_send()
        b_left.wait_recv()

    def send_home(part, k):
        t = 4 * ((t_i // 4 + k // 4) % 2) + (t_i + k) % 4
        fields = pl.ds(0, 3) if part == 0 else pl.ds(3, 7)
        return remote(
            OB.at[fields, pl.ds(32 * t, 32), :],
            o_planes.at[fields, pl.ds(32 * d, 32), :],
            o_send.at[part, k],
            o_recv,
            (role, t),
        )

    homes = [[send_home(part, k) for k in (0, 4, 6, 5, 7, 1, 3, 2)] for part in range(2)]

    def start_home(part):
        for copy in homes[part][1:]:
            copy.start()
        pl.when(swapped)(homes[part][0].start)
        fields = pl.ds(0, 3) if part == 0 else pl.ds(3, 7)

        @pl.when(jnp.logical_not(swapped))
        def _():
            pltpu.make_async_copy(
                OB.at[fields, pl.ds(32 * t_i, 32), :], o_planes.at[fields, pl.ds(32 * d, 32), :], o_recv
            ).start()

    def velocities_home():
        for z in range(32):
            rows = pl.ds(z, 8, stride=32)
            for j, f in enumerate(VELOCITY):
                OB[f, rows, :] = V[j, 4 + z]
        start_home(0)

    def rest_home():
        for z in range(32):
            rows = pl.ds(z, 8, stride=32)
            for j, f in enumerate(WITH_Z):
                OB[f, rows, :] = SZ[j, 4 + z]
            for j, f in enumerate(IN_PLANE):
                OB[f, rows, :] = SO[j, z]
            OB[9, rows, :] = IMG[z] * UNIT
        start_home(1)

    def step(n, carry):
        par = lax.rem(n, 2)
        amplitude = PR[pl.ds(n, 1), :]
        for z0 in (4, 12, 20):
            inner_velocity(z0, amplitude)
        wait_halo(par)
        complete_velocity(par)
        pl.when(n == STEPS - 1)(velocities_home)
        for z0 in (0, 24):
            stresses(z0)

        @pl.when(n < STEPS - 1)
        def _():
            start_halo(1 - par, 0)
            partial_velocity(1 - par, PR[pl.ds(n + 1, 1), :])
            start_halo(1 - par, 1)

        for z0 in (8, 16):
            stresses(z0)
        pl.when(n == STEPS - 1)(rest_home)
        picked = jnp.dot(R1[...], split(V[2, 4:36].reshape(256, 128)), preferred_element_type=F32)
        picked = (picked * L2[...]).astype(BF16)
        TRB[n] = lax.dot_general(
            jnp.ones((8, 256), BF16), picked, (((1,), (1,)), ((), ())), preferred_element_type=F32
        )
        pl.when(n == 1)(start_gradients)
        pl.when(n == 5)(gradients)
        return carry

    lax.fori_loop(0, STEPS, step, 0)

    for n in range(STEPS):
        TRS[n : n + 1, :] = TRB[n, 0:1, :]

    def send_trace(k):
        return remote(TRS, TRR.at[d], t_send.at[k], t_recv, (role, (t_i + k) % 8))

    traces = [send_trace(k) for k in range(8)]
    for copy in traces[1:]:
        copy.start()
    pl.when(swapped)(traces[0].start)

    @pl.when(jnp.logical_not(swapped))
    def _():
        pltpu.make_async_copy(TRS, TRR.at[d], t_recv).start()


    for copies in (spread, grads, owners, waves):
        for copy in copies:
            copy.wait_send()
    pl.when(swapped)(wave_near.wait_send)
    for k in range(1, 16):
        deliver[k].wait_send()
    pl.when(elsewhere)(deliver[0].wait_send)
    pltpu.make_async_copy(o_owner, o_owner, h_recv).wait()

    pltpu.make_async_copy(TRR, TRR, t_recv).wait()
    total = TRR[0]
    for j in range(1, 8):
        total = total + TRR[j]
    o_trace[...] = total

    pltpu.make_async_copy(o_planes, o_planes, o_recv).wait()
    for copy in homes[0][1:] + homes[1][1:] + traces[1:]:
        copy.wait_send()

    @pl.when(swapped)
    def _():
        for copy in (homes[0][0], homes[1][0], traces[0]):
            copy.wait_send()


def finish(planes, owner, trace, o_state, o_image, o_owner, o_trace):
    for f in range(9):
        o_state[f] = planes[f].T
    o_image[...] = planes[9].T
    o_owner[...] = owner[...]
    for n in range(STEPS):
        o_trace[n] = trace[n : n + 1, :]


def on_device(
    lame_lambda, lame_mu, buoyancy, aperture_row, wave_state, source_cell, wavelet, receiver_cell,
    prev_row, prev_grad,
):
    weights = jnp.asarray(operators(), BF16)
    vmem = pl.BlockSpec(memory_space=pltpu.VMEM)
    smem = pl.BlockSpec(memory_space=pltpu.SMEM)
    dma = pltpu.SemaphoreType.DMA
    tile = (8, 128)
    planes, owner, trace = pl.pallas_call(
        kernel,
        out_shape=(
            jax.ShapeDtypeStruct((10, 256, 128), F32),
            jax.ShapeDtypeStruct((128, 256), F32),
            jax.ShapeDtypeStruct((STEPS, 256), F32),
        ),
        in_specs=[smem] * 4 + [vmem] + [pl.BlockSpec(memory_space=pl.ANY)] * 6,
        out_specs=(pl.BlockSpec(memory_space=pl.ANY), vmem, vmem),
        scratch_shapes=[
            pltpu.VMEM((9, 128, 256), F32),
            pltpu.VMEM((3, 128, 256), F32),
            pltpu.VMEM((128, 256), F32),
            pltpu.VMEM((256, 512), BF16),
            pltpu.VMEM((9, 256, 128), F32),
            pltpu.VMEM((9, 256, 128), F32),
            pltpu.VMEM((3, 256, 128), F32),
            pltpu.VMEM((16, 3, 16, 128), F32),
            pltpu.VMEM((16, 3, 16, 128), F32),
            pltpu.VMEM((3, 256, 128), F32),
            pltpu.VMEM((16, 8, 256), F32),
            pltpu.VMEM((16, 8, 256), F32),
            pltpu.VMEM((24, 128), F32),
            pltpu.VMEM((24, 128), F32),
            pltpu.VMEM((24, 128), F32),
            pltpu.VMEM((3, 40) + tile, F32),
            pltpu.VMEM((3, 32) + tile, F32),
            pltpu.VMEM((3, 40) + tile, F32),
            pltpu.VMEM((40,) + tile, F32),
            pltpu.VMEM((32,) + tile, F32),
            pltpu.VMEM((32,) + tile, F32),
            pltpu.VMEM((32,) + tile, F32),
            pltpu.VMEM((32,) + tile, F32),
            pltpu.VMEM((32,) + tile, F32),
            pltpu.VMEM((2, 2, 3, 4) + tile, F32),
            pltpu.VMEM((2, 2, 3, 4) + tile, F32),
            pltpu.VMEM((2, 2, 3, 4) + tile, F32),
            pltpu.VMEM((256, 256), BF16),
            pltpu.VMEM((256, 256), F32),
            pltpu.VMEM((STEPS, 8, 256), F32),
            pltpu.VMEM((STEPS, 256), F32),
            pltpu.VMEM((8, STEPS, 256), F32),
            pltpu.VMEM((10, 256, 128), F32),
            dma((6,)), dma((8,)), dma, dma((16,)), dma, dma((16,)), dma, dma((16,)), dma, dma((16,)), dma,
            dma, dma, dma((2, 2, 2)), dma((2, 2, 2)), dma((2,)), dma((2,)), dma((8,)), dma, dma((2, 8)), dma,
        ],
        compiler_params=pltpu.CompilerParams(collective_id=0, has_side_effects=True),
        name="wave",
    )(
        aperture_row,
        prev_row,
        source_cell,
        wavelet,
        receiver_cell,
        wave_state.reshape(9, 128, 256),
        lame_lambda.reshape(128, 256),
        lame_mu.reshape(128, 256),
        buoyancy.reshape(128, 256),
        prev_grad.reshape(128, 256),
        weights,
    )
    state, image, owner, trace = pl.pallas_call(
        finish,
        out_shape=(
            jax.ShapeDtypeStruct((9, 128, 256), F32),
            jax.ShapeDtypeStruct((128, 256), F32),
            jax.ShapeDtypeStruct((128, 256), F32),
            jax.ShapeDtypeStruct((STEPS, 1, 256), F32),
        ),
        in_specs=[vmem] * 3,
        out_specs=(vmem,) * 4,
        name="finish",
    )(planes, owner, trace)
    return (
        state.reshape(1, 9, 4, 32, 256),
        image.reshape(1, 4, 32, 256),
        owner.reshape(4, 32, 256),
        jnp.transpose(trace, (1, 0, 2)),
    )


def solution(mesh):
    placed = (
        P(("shot", "tile"), None, None),
        P(("shot", "tile"), None, None),
        P(("shot", "tile"), None, None),
        P(),
        P("shot", None, "tile", None, None),
        P("shot"),
        P("shot", None),
        P("shot", None),
        P(),
        P("shot", "tile", None, None),
    )
    return jax.shard_map(
        on_device,
        mesh=mesh,
        in_specs=placed,
        out_specs=(
            P("shot", None, "tile", None, None),
            P("shot", "tile", None, None),
            P(("shot", "tile"), None, None),
            P("shot", None, None),
        ),
        check_vma=False,
    )
```
